512 devices in a mesh: ctx: 32 (over z, core), ch: 16 (over x, y).
Axes of the slice: x: 4, y: 4, z: 16, core: 2. Of those that a mesh axis runs over, the one named last changes fastest.
Arguments:
- query_in: bfloat16 [8192, 4096], P('ctx', 'ch'), may hold values from -63 to 63
- key_in: bfloat16 [8192, 4096], P('ctx', 'ch'), may hold values from -4 to 4
- value_in: bfloat16 [8192, 4096], P('ctx', 'ch'), may hold values from -4 to 4
- short_taps: float32 [7, 3, 4096], P(None, None, 'ch'), may hold values from -2 to 2
- residues: float32 [4096, 16], P('ch'), may hold values from -1.5 to 1.5
- decays: float32 [4096, 16], P('ch'), may hold values from 6.1035157e-06 to 0.02
- out_weight: bfloat16 [4096, 4096], P('ch'), may hold values from -0.125 to 0.125
- out_grad: bfloat16 [8192, 4096], P('ctx', 'ch'), may hold values from -6 to 6
Outputs:
- projected: bfloat16 [8192, 4096], P('ctx', 'ch')
- grad_query: bfloat16 [8192, 4096], P('ctx', 'ch')
- grad_key: bfloat16 [8192, 4096], P('ctx', 'ch')
- grad_value: bfloat16 [8192, 4096], P('ctx', 'ch')
The draws below stay inside these ranges and needn't reach their ends.
All inputs are finite; a program needn't handle non-finite values.
Results may differ from the reference program's by a relative error of at most 0.0058.
Values may be sent and summed in bfloat16 or wider, within the bound.
A program may use at most 64 MiB of HBM per device.

```python
import math
import jax
import jax.numpy as jnp
import numpy as np
from jax import lax

D = 4096
MODES = 16
KERNEL = 7
SEQ = 8192


def offset_field(key, salt):
    base_key = jax.random.fold_in(key, salt)
    values = jnp.clip(jax.random.normal(base_key, (SEQ, D), jnp.float32), -4.0, 4.0)
    return values.astype(jnp.bfloat16)


def draw_query_in(key, part):
    streams = jax.random.split(jax.random.fold_in(key, 11), 3)
    base_vals = jnp.clip(jax.random.normal(streams[0], (SEQ, D), jnp.float32), -4.0, 4.0)
    trend_span = 3.0
    position = jnp.arange(D, dtype=jnp.float32) / D - 0.5
    column_scale = jnp.exp(jax.random.uniform(streams[1], (D,), jnp.float32, math.log(0.3), math.log(3.0)))
    column_scale = column_scale * jnp.exp(math.log(trend_span) * position)
    row_scale = jnp.exp(jax.random.uniform(streams[2], (SEQ, 1), jnp.float32, math.log(0.3), math.log(3.0)))
    return (base_vals * column_scale * row_scale).astype(jnp.bfloat16)


def draw_key_in(key, part):
    return offset_field(key, 23)


def draw_value_in(key, part):
    return offset_field(key, 37)


def with_spikes(entries, own_key, source, target, blocks, factor):
    owner, partner = [(jnp.arange(entries.shape[dim]) // (entries.shape[dim] // blocks)).reshape([-1 if axis == dim else 1 for axis in range(entries.ndim)]) for dim in (source, target)]
    chosen = jax.random.permutation(own_key, blocks)[partner]
    strong = (owner == chosen) | (owner == (partner + blocks // 2) % blocks)
    return jnp.where(strong, factor * entries, entries)


def level_of(rng, extent, cuts, smallest, top_value):
    loudness = 1.0
    for dim, parts in cuts:
        draws = jax.random.uniform(jax.random.fold_in(jax.random.fold_in(rng, 6), dim), (parts,), jnp.float32, smallest / len(cuts), top_value / len(cuts))
        loudness = loudness * jnp.repeat(jnp.exp(draws), extent[dim] // parts).reshape((-1,) + (1,) * (len(extent) - 1 - dim))
    return loudness


def normal_values(own_key, extent, deviation, limit, cuts=(), kind=jnp.bfloat16):
    array = deviation * jax.random.normal(own_key, extent, jnp.float32)
    if cuts:
        array = array * level_of(own_key, extent, cuts, -0.22, 0.18)
    return jnp.clip(array, -limit, limit).astype(kind)


def gaussian_with(key, dims, width, most, cuts, heavy, kind=jnp.bfloat16):
    entries = width * jax.random.normal(key, dims, jnp.float32)
    if cuts:
        entries = entries * level_of(key, dims, cuts, -0.22, 0.18)
    return jnp.clip(with_spikes(entries, jax.random.fold_in(key, 3), *heavy), -most, most).astype(kind)


def setup_inputs(seed: int = 0) -> dict:
    keys = jax.random.split(jax.random.key(seed), 9)
    query_in = draw_query_in(jax.random.fold_in(keys[8], 71), 0)
    key_in = draw_key_in(jax.random.fold_in(keys[8], 71), 0)
    value_in = draw_value_in(jax.random.fold_in(keys[8], 71), 0)
    short_taps = normal_values(keys[3], (KERNEL, 3, D), KERNEL ** -0.5, 2.0, ((2, 16),), jnp.float32)
    residues = normal_values(keys[4], (D, MODES), MODES ** -0.5, 1.5, ((0, 16),), jnp.float32)
    decays = jnp.clip(jnp.exp(math.log(0.02) - 8.094623 * jax.random.uniform(keys[5], (D, MODES), jnp.float32) ** level_of(keys[5], (D, MODES), ((0, 16),), -0.2, 0.2)), 6.10351571594947e-06, 0.02)
    out_weight = gaussian_with(keys[6], (D, D), D ** -0.5, 0.125, ((0, 16),), (0, 1, 16, 2.0))
    out_grad = normal_values(keys[7], (SEQ, D), 1.0, 6.0, ((0, 32), (1, 16)))
    return {"query_in": query_in, "key_in": key_in, "value_in": value_in, "short_taps": short_taps, "residues": residues, "decays": decays, "out_weight": out_weight, "out_grad": out_grad}


block_len = 64
exact_precision = lax.Precision.HIGHEST

def featurize(signal, taps):
    kernel_len = taps.shape[0]
    length = signal.shape[0]
    padded = jnp.pad(signal, ((kernel_len - 1, 0), (0, 0)))
    final_output = jnp.zeros_like(signal)
    for tap_index in range(kernel_len):
        begin = kernel_len - 1 - tap_index
        final_output = final_output + taps[tap_index] * padded[begin:begin + length]
    return final_output

def featurize_back(grads_in, taps):
    kernel_len = taps.shape[0]
    length = grads_in.shape[0]
    padded = jnp.pad(grads_in, ((0, kernel_len - 1), (0, 0)))
    final_output = jnp.zeros_like(grads_in)
    for tap_index in range(kernel_len):
        final_output = final_output + taps[tap_index] * padded[tap_index:tap_index + length]
    return final_output

def modal_conv(signal, residues, decays):
    channels, length = signal.shape
    pieces = length // block_len
    offsets = jnp.arange(block_len, dtype=jnp.float32)
    scaled = residues * jnp.sqrt(decays)
    filter_head = jnp.einsum('cn,cnd->cd', scaled, jnp.exp(-decays[:, :, None] * offsets), precision=exact_precision)
    indices = np.arange(block_len)
    distance = indices[:, None] - indices[None, :]
    toeplitz = jnp.where(jnp.asarray(distance >= 0)[None], filter_head[:, np.maximum(distance, 0)], 0.0)
    decay_in = jnp.exp(-decays[:, :, None] * (block_len - 1.0 - offsets))
    decay_out = scaled[:, :, None] * jnp.exp(-decays[:, :, None] * (offsets + 1.0))
    step_decay = jnp.exp(-decays * block_len)
    block_list = jnp.transpose(signal.reshape(channels, pieces, block_len), (1, 0, 2))

    def advance(carried_state, segment):
        produced = jnp.einsum('cij,cj->ci', toeplitz, segment, precision=exact_precision)
        produced = produced + jnp.einsum('cn,cni->ci', carried_state, decay_out, precision=exact_precision)
        carried_state = carried_state * step_decay + jnp.einsum('cj,cnj->cn', segment, decay_in, precision=exact_precision)
        return (carried_state, produced)
    _, outputs = lax.scan(advance, jnp.zeros(decays.shape, jnp.float32), block_list)
    return jnp.transpose(outputs, (1, 0, 2)).reshape(channels, length)

def reference(query_in, key_in, value_in, short_taps, residues, decays, out_weight, out_grad):
    query_feat = featurize(query_in.astype(jnp.float32), short_taps[:, 0])
    key_feat = featurize(key_in.astype(jnp.float32), short_taps[:, 1])
    value_feat = featurize(value_in.astype(jnp.float32), short_taps[:, 2])
    mixed_values = (key_feat * value_feat).astype(jnp.bfloat16)
    mixed_wide = lax.optimization_barrier(mixed_values).astype(jnp.float32)
    conv_out = modal_conv(mixed_wide.T, residues, decays).T
    gated = (query_feat * conv_out).astype(jnp.bfloat16)
    projected = jnp.dot(gated, out_weight, preferred_element_type=jnp.float32).astype(jnp.bfloat16)
    grad_gated = jnp.dot(out_grad, out_weight.T, preferred_element_type=jnp.float32)
    grad_query_feat = (grad_gated * conv_out).astype(jnp.bfloat16)
    grad_mixed = (grad_gated * query_feat).astype(jnp.bfloat16)
    grad_wide = lax.optimization_barrier(grad_mixed).astype(jnp.float32)
    grad_conv = jnp.flip(modal_conv(jnp.flip(grad_wide.T, 1), residues, decays), 1).T
    grad_key_feat = (grad_conv * value_feat).astype(jnp.bfloat16)
    grad_value_feat = (grad_conv * key_feat).astype(jnp.bfloat16)
    grad_query = featurize_back(grad_query_feat.astype(jnp.float32), short_taps[:, 0]).astype(jnp.bfloat16)
    grad_key = featurize_back(grad_key_feat.astype(jnp.float32), short_taps[:, 1]).astype(jnp.bfloat16)
    grad_value = featurize_back(grad_value_feat.astype(jnp.float32), short_taps[:, 2]).astype(jnp.bfloat16)
    return (projected, grad_query, grad_key, grad_value)
```

```python
import functools

import jax
import jax.numpy as jnp
from jax import lax
from jax.experimental import pallas as pl
from jax.experimental.pallas import tpu as pltpu
from jax.sharding import PartitionSpec as P

MESH = pl.DeviceIdType.MESH
F32 = jnp.float32
BF16 = jnp.bfloat16
SIDE = 4
SUB = 8
LANES = 128
AG_COPIES = 44
RS_COPIES = 60


def kernel(
    chips,
    modes,
    taps_len,
    q_in,
    k_in,
    v_in,
    taps_in,
    res_in,
    dec_in,
    w_in,
    g_in,
    proj_out,
    gq_out,
    gk_out,
    gv_out,
    raw,
    taps,
    res,
    dec,
    weight,
    gathered,
    halo,
    natural,
    extended,
    feats,
    signal,
    conv,
    gradient,
    filt,
    small,
    rates,
    decay,
    scan_buf,
    prefix,
    s_send,
    s_recv,
    x_send,
    x_recv,
    carry,
    gate,
    keep0,
    keep1,
    send_a,
    send_p,
    send_b,
    recv_a,
    recv_p,
    recv_b,
    part2,
    own2,
    send2_b,
    recv2_a,
    recv2_p,
    recv2_b,
    gfeats,
    edge_send,
    edge_recv,
    outs,
    local_sem,
    ag_send,
    ag_recv,
    rs_send,
    rs_recv,
    z_send,
    z_recv,
    p_send,
    p_recv,
    h_send,
    h_recv,
    e_send,
    e_recv,
    out_sem,
):
    length, width = q_in.shape
    rows = length // SUB
    half = length // 2
    quarter = length // 4
    lanes = range(width // LANES)
    ctx = lax.axis_index("ctx")
    ch = lax.axis_index("ch")
    z, core = ctx // 2, ctx % 2
    x, y = ch // SIDE, ch % SIDE
    n_ctx = 2 * chips
    before = (ctx + n_ctx - 1) % n_ctx
    after = (ctx + 1) % n_ctx
    partner = z * 2 + (1 - core)

    def plane(axis, step):
        if axis == 0:
            other = ((x + step) % SIDE) * SIDE + y
        else:
            other = x * SIDE + (y + step) % SIDE
        return {"ctx": ctx, "ch": other}

    def along_z(step):
        return {"ctx": ((z + step) % chips) * 2 + core, "ch": ch}

    def at_ctx(other):
        return {"ctx": other, "ch": ch}

    local = [
        pltpu.make_async_copy(dec_in, dec, local_sem.at[0]),
        pltpu.make_async_copy(res_in, res, local_sem.at[1]),
        pltpu.make_async_copy(taps_in, taps, local_sem.at[2]),
        pltpu.make_async_copy(q_in, raw.at[0], local_sem.at[3]),
        pltpu.make_async_copy(k_in, raw.at[1], local_sem.at[4]),
        pltpu.make_async_copy(v_in, raw.at[2], local_sem.at[5]),
        pltpu.make_async_copy(g_in, gathered.at[0, 0], local_sem.at[6]),
        pltpu.make_async_copy(w_in, weight, local_sem.at[7]),
    ]
    for copy in local:
        copy.start()

    barrier = pltpu.get_barrier_semaphore()
    peers = [plane(0, 1), plane(0, -1), plane(1, 1), plane(1, -1), at_ctx(before), at_ctx(after)]
    peers += [along_z(step) for step in range(1, chips)]
    for peer in peers:
        pl.semaphore_signal(barrier, inc=1, device_id=peer, device_id_type=MESH)
    pl.semaphore_wait(barrier, len(peers))

    def remote(src, dst, sends, recvs, index, device):
        return pltpu.make_async_remote_copy(
            src_ref=src,
            dst_ref=dst,
            send_sem=sends.at[index],
            recv_sem=recvs.at[index],
            device_id=device,
            device_id_type=MESH,
        )

    ag = {}

    def slot(h, i, j):
        return gathered.at[i, j] if h == 0 else gathered.at[j, i]

    def piece(ref, h, part):
        if part is None:
            return ref.at[pl.ds(h * half, half)]
        return ref.at[pl.ds(h * half + part * quarter, quarter)]

    def ag_copy(h, phase, source, i, j, part, step):
        key = (h, i, j, part, step)
        index = len(ag)
        axis = phase if h == 0 else 1 - phase
        copy = remote(
            piece(source, h, part), piece(slot(h, i, j), h, part), ag_send, ag_recv, index, plane(axis, step)
        )
        ag[key] = copy
        copy.start()

    def ag_wait(h, i, j, part, step):
        ag[(h, i, j, part, step)].wait_recv()

    for h in range(2):
        for step in (1, -1):
            ag_copy(h, 0, g_in, step % SIDE, 0, None, step)
    for s in range(3):
        remote(
            (q_in, k_in, v_in)[s].at[pl.ds(length - 16, 16)], halo.at[s], h_send, h_recv, s, at_ctx(after)
        ).start()
    for h in range(2):
        for step in (1, -1):
            ag_copy(h, 1, g_in, 0, step % SIDE, None, step)

    def ag_relay1():
        for h in range(2):
            for step in (1, -1):
                i = step % SIDE
                ag_wait(h, i, 0, None, step)
                ag_copy(h, 0, slot(h, i, 0), 2, 0, 0 if step == 1 else 1, step)
        for h in range(2):
            for i in (1, 3):
                for step in (1, -1):
                    ag_copy(h, 1, slot(h, i, 0), i, step % SIDE, None, step)

    def ag_relay2(i):
        for h in range(2):
            for step in (1, -1):
                j = step % SIDE
                ag_wait(h, i, j, None, step)
                ag_copy(h, 1, slot(h, i, j), i, 2, 0 if step == 1 else 1, step)

    def ag_far():
        for h in range(2):
            for part, step in ((0, 1), (1, -1)):
                ag_wait(h, 2, 0, part, step)
                for to in (1, -1):
                    ag_copy(h, 1, slot(h, 2, 0), 2, to % SIDE, part, to)

    def ag_relay_far():
        for h in range(2):
            for step in (1, -1):
                part = 0 if step == 1 else 1
                ag_wait(h, 2, step % SIDE, part, step)
                ag_copy(h, 1, slot(h, 2, step % SIDE), 2, 2, part, step)

    def ag_last():
        for h in range(2):
            for step in (1, -1):
                ag_wait(h, 2, step % SIDE, 1 if step == 1 else 0, step)
        for i in (0, 1, 3, 2):
            for h in range(2):
                for part, step in ((0, 1), (1, -1)):
                    ag_wait(h, i, 2, part, step)

    local[0].wait()
    local[1].wait()
    rates[0] = jnp.transpose(dec[...])
    rates[1] = jnp.transpose(res[...])
    rate = rates[0]
    scale = rates[1] * jnp.sqrt(rate)
    rates[1] = scale
    offsets = lax.broadcasted_iota(jnp.int32, (rows, width), 0).astype(F32)
    total = jnp.zeros((rows, width), F32)
    for n in range(modes):
        total = total + rates[1, n : n + 1, :] * jnp.exp(-rates[0, n : n + 1, :] * offsets)
    small[...] = total
    for d in range(rows):
        filt[d] = jnp.broadcast_to(small[d : d + 1, :], (SUB, width))
    for n in range(modes):
        own = jnp.broadcast_to(rates[0, n : n + 1, :], (SUB, width))
        decay[6, n] = jnp.broadcast_to(rates[1, n : n + 1, :], (SUB, width))
        decay[0, n] = jnp.exp(-own)
        step_decay = jnp.exp(-own * rows)
        decay[1, n] = step_decay
        step_decay = step_decay * step_decay
        decay[2, n] = step_decay
        step_decay = step_decay * step_decay
        decay[3, n] = step_decay
        place = lax.broadcasted_iota(jnp.int32, (SUB, width), 0)
        decay[4, n] = jnp.exp(-own * (rows * place).astype(F32))
        decay[5, n] = jnp.exp(-own * (rows * (SUB - 1 - place)).astype(F32))
    block_decay = jnp.exp(-rate * length)
    pair_decay = jnp.exp(-rate * (2 * length))
    sublane = lax.broadcasted_iota(jnp.int32, (modes, SUB, width), 1)

    def states(signal, direction):
        def advance(r, total):
            at = r if direction == 1 else rows - 1 - r
            return total * decay[0] + signal[at][None]

        total = lax.fori_loop(0, rows, advance, jnp.zeros((modes, SUB, width), F32))
        for level, step in enumerate((1, 2, 4)):
            if direction == 1:
                moved = jnp.where(sublane >= step, pltpu.roll(total, step, 1), 0.0)
            else:
                moved = jnp.where(sublane < SUB - step, pltpu.roll(total, SUB - step, 1), 0.0)
            total = total + decay[1 + level] * moved
        if direction == 1:
            prefix[...] = jnp.where(sublane >= 1, pltpu.roll(total, 1, 1), 0.0)
        else:
            prefix[...] = jnp.where(sublane < SUB - 1, pltpu.roll(total, SUB - 1, 1), 0.0)
        scan_buf[...] = total
        edge = SUB - 1 if direction == 1 else 0
        for n in range(modes):
            carry[0, n : n + 1, :] = scan_buf[n, edge : edge + 1, :]

    def send_states(way, direction):
        s_send[way] = carry[0].astype(BF16)
        for step in range(chips // 2, 0, -1):
            for distance in {step, chips - step}:
                remote(
                    s_send.at[way],
                    s_recv.at[way, distance],
                    z_send.at[way],
                    z_recv.at[way],
                    distance,
                    along_z(direction * distance),
                ).start()

    def take_states(way, direction):
        total = jnp.zeros((modes, width), F32)
        for distance in range(chips - 1, 0, -1):
            remote(
                s_send.at[way],
                s_recv.at[way, distance],
                z_send.at[way],
                z_recv.at[way],
                distance,
                along_z(direction * distance),
            ).wait_recv()
            source = z - distance if direction == 1 else chips - 1 - z - distance
            there = (source >= 0).astype(F32)
            total = total * pair_decay + there * s_recv[way, distance].astype(F32)
        leads = (core == 0) if direction == 1 else (core == 1)
        leads = leads.astype(F32)
        x_send[way] = leads * (pair_decay * total + carry[0]) + (1.0 - leads) * total
        copy = remote(x_send.at[way], x_recv.at[way], p_send, p_recv, way, at_ctx(partner))
        copy.start()
        carry[1] = block_decay * total

    def finish_states(way):
        remote(x_send.at[way], x_recv.at[way], p_send, p_recv, way, at_ctx(partner)).wait_recv()
        carry[1] = carry[1] + x_recv[way]
        for n in range(modes):
            scan_buf[n] = jnp.broadcast_to(carry[1, n : n + 1, :], (SUB, width))

    def carried(out, direction):
        reach = decay[4] if direction == 1 else decay[5]
        start = decay[6] * decay[0] * (prefix[...] + reach * scan_buf[...])

        def advance(r, state):
            at = r if direction == 1 else rows - 1 - r
            out[at] = out[at] + jnp.sum(state, axis=0)
            return state * decay[0]

        lax.fori_loop(0, rows, advance, start)

    ag_relay1()
    for index in (2, 3, 4, 5):
        local[index].wait()
    first = (ctx > 0).astype(F32)
    for s in range(3):
        remote(
            (q_in, k_in, v_in)[s].at[pl.ds(length - 16, 16)], halo.at[s], h_send, h_recv, s, at_ctx(after)
        ).wait_recv()
        for g in lanes:
            cols = slice(g * LANES, (g + 1) * LANES)
            natural[s, g, 8 : 8 + length] = raw[s, :, cols].astype(F32)
            natural[s, g, 0:8] = halo[s, :, cols].astype(F32)[8:16] * first
            for i in range(8 - taps_len + 1, 8 + rows):
                extended[s, i, :, cols] = natural[s, g, pl.ds(i, SUB, stride=rows), :]
        total = jnp.zeros((rows, SUB, width), F32)
        for j in range(taps_len):
            total = total + taps[j, s : s + 1, :][None] * extended[s, 8 - j : 8 - j + rows]
        feats[s] = total
    signal[...] = (feats[1] * feats[2]).astype(BF16).astype(F32)

    states(signal, 1)
    send_states(0, 1)
    ag_relay2(0)
    ag_far()
    conv[0] = filt[0][None] * signal[...]
    for d in range(1, rows):
        conv[0, d:rows] = conv[0, d:rows] + filt[d][None] * signal[0 : rows - d]
    ag_relay2(1)
    ag_relay2(3)
    ag_relay_far()
    take_states(0, 1)
    finish_states(0)
    carried(conv.at[0], 1)
    gate[...] = (feats[0] * conv[0]).astype(BF16).reshape(length, width)

    local[7].wait()
    rs = {}

    def rs_copy(key, src, dst, axis, step):
        copy = remote(src, dst, rs_send, rs_recv, len(rs), plane(axis, step))
        rs[key] = copy
        copy.start()

    def first_axis(h):
        return 1 if h == 0 else 0

    lower, upper = pl.ds(0, quarter), pl.ds(quarter, quarter)

    def terms(dx, dy):
        dest = ((x + dx) % SIDE) * SIDE + (y + dy) % SIDE
        product = jnp.dot(
            gate[...],
            weight[:, pl.ds(pl.multiple_of(dest * width, width), width)],
            preferred_element_type=F32,
        )
        for h in range(2):
            i, j = (dx, dy) if h == 0 else (dy, dx)
            own = product[h * half : (h + 1) * half]
            if j == 2:
                send_a[h, i] = own.astype(BF16)
                rs_copy(("a", h, i, 0), send_a.at[h, i, lower], recv_a.at[h, 0, i], first_axis(h), 1)
                rs_copy(("a", h, i, 1), send_a.at[h, i, upper], recv_a.at[h, 1, i], first_axis(h), -1)
            elif j == 1:
                keep1[h, 0, i] = own[:quarter]
                send_p[h, 0, i] = own[quarter:].astype(BF16)
            elif j == 3:
                keep1[h, 1, i] = own[quarter:]
                send_p[h, 1, i] = own[:quarter].astype(BF16)
            else:
                keep0[h, i] = own

    for dx, dy in ((2, 2), (2, 1), (1, 2), (2, 3), (3, 2), (2, 0), (0, 2)):
        terms(dx, dy)
    for dx, dy in ((1, 1), (1, 3), (3, 1), (3, 3), (0, 1), (1, 0), (0, 3), (3, 0), (0, 0)):
        terms(dx, dy)

    ag_last()
    local[6].wait()
    grad = jnp.zeros((length, width), F32)
    for dx in range(SIDE):
        for dy in range(SIDE):
            source = ((x + SIDE - dx) % SIDE) * SIDE + (y + SIDE - dy) % SIDE
            grad = grad + lax.dot_general(
                gathered[dx, dy],
                weight[:, pl.ds(pl.multiple_of(source * width, width), width)],
                (((1,), (1,)), ((), ())),
                preferred_element_type=F32,
            )
    for g in lanes:
        cols = slice(g * LANES, (g + 1) * LANES)
        natural[0, g, 0:length] = grad[:, cols]
        for r in range(rows):
            gradient[r, :, cols] = natural[0, g, pl.ds(r, SUB, stride=rows), :]
    signal[...] = (gradient[...] * feats[0]).astype(BF16).astype(F32)
    states(signal, -1)
    send_states(1, -1)

    for h in range(2):
        for i in (2, 1, 3, 0):
            rs_copy(("p", h, i, 0), send_p.at[h, 0, i], recv_p.at[h, 0, i], first_axis(h), 1)
            rs_copy(("p", h, i, 1), send_p.at[h, 1, i], recv_p.at[h, 1, i], first_axis(h), -1)

    def rs_second():
        for i in (2, 1, 3, 0):
            for h in range(2):
                for way, step in ((0, 1), (1, -1)):
                    rs[("a", h, i, way)].wait_recv()
                    send_b[h, way, i] = (keep1[h, way, i] + recv_a[h, way, i].astype(F32)).astype(BF16)
                    rs_copy(("b", h, i, way), send_b.at[h, way, i], recv_b.at[h, way, i], first_axis(h), step)

    rs_second()

    conv[1] = filt[0][None] * signal[...]
    for d in range(1, rows):
        conv[1, 0 : rows - d] = conv[1, 0 : rows - d] + filt[d][None] * signal[d:rows]

    def edges(s):
        for j in range(16):
            small[j : j + 1, :] = gfeats[s, j, 0:1, :]
        edge_send[s] = small[0:16].astype(BF16)
        remote(edge_send.at[s], edge_recv.at[s], e_send, e_recv, s, at_ctx(before)).start()

    gfeats[0, 0:rows] = (gradient[...] * conv[0]).astype(BF16).astype(F32)
    edges(0)

    def collect(h, i):
        for way in range(2):
            rs[("p", h, i, way)].wait_recv()
            rs[("b", h, i, way)].wait_recv()
        low = keep0[h, i, 0:quarter] + recv_b[h, 0, i].astype(F32) + recv_p[h, 1, i].astype(F32)
        high = keep0[h, i, quarter:half] + recv_p[h, 0, i].astype(F32) + recv_b[h, 1, i].astype(F32)
        return low, high

    for h in range(2):
        axis = 1 - first_axis(h)
        low, high = collect(h, 2)
        part2[h, 0] = low.astype(BF16)
        part2[h, 1] = high.astype(BF16)
        rs_copy(("a2", h, 0), part2.at[h, 0], recv2_a.at[h, 0], axis, 1)
        rs_copy(("a2", h, 1), part2.at[h, 1], recv2_a.at[h, 1], axis, -1)
    for h in range(2):
        axis = 1 - first_axis(h)
        low, high = collect(h, 1)
        own2[h, 0] = low
        part2[h, 2] = high.astype(BF16)
        rs_copy(("p2", h, 0), part2.at[h, 2], recv2_p.at[h, 0], axis, 1)
        low, high = collect(h, 3)
        own2[h, 1] = high
        part2[h, 3] = low.astype(BF16)
        rs_copy(("p2", h, 1), part2.at[h, 3], recv2_p.at[h, 1], axis, -1)
    for h in range(2):
        axis = 1 - first_axis(h)
        low, high = collect(h, 0)
        own2[h, 2] = low
        own2[h, 3] = high
        for way, step in ((0, 1), (1, -1)):
            rs[("a2", h, way)].wait_recv()
            send2_b[h, way] = (own2[h, way] + recv2_a[h, way].astype(F32)).astype(BF16)
            rs_copy(("b2", h, way), send2_b.at[h, way], recv2_b.at[h, way], axis, step)

    take_states(1, -1)
    finish_states(1)
    carried(conv.at[1], -1)
    gfeats[1, 0:rows] = (conv[1] * feats[2]).astype(BF16).astype(F32)
    edges(1)
    gfeats[2, 0:rows] = (conv[1] * feats[1]).astype(BF16).astype(F32)
    edges(2)

    for h in range(2):
        for way in range(2):
            rs[("p2", h, way)].wait_recv()
            rs[("b2", h, way)].wait_recv()
        low = own2[h, 2] + recv2_b[h, 0].astype(F32) + recv2_p[h, 1].astype(F32)
        high = own2[h, 3] + recv2_p[h, 0].astype(F32) + recv2_b[h, 1].astype(F32)
        per = quarter // SUB
        for piece_index, value in ((2 * h, low), (2 * h + 1, high)):
            value = value.reshape(per, SUB, width)
            for g in lanes:
                for r in range(per):
                    natural[1, g, pl.ds(piece_index * per + r, SUB, stride=rows), :] = value[
                        r, :, g * LANES : (g + 1) * LANES
                    ]
    for g in lanes:
        outs[0, :, g * LANES : (g + 1) * LANES] = natural[1, g, 0:length].astype(BF16)
    out_copies = [pltpu.make_async_copy(outs.at[0], proj_out, out_sem.at[0])]
    out_copies[0].start()

    last = (ctx < n_ctx - 1).astype(F32)
    place = lax.broadcasted_iota(jnp.int32, (SUB, width), 0)
    for s in range(3):
        remote(edge_send.at[s], edge_recv.at[s], e_send, e_recv, s, at_ctx(before)).wait_recv()
        small[0:16] = edge_recv[s].astype(F32) * last
        for j in range(taps_len - 1):
            moved = pltpu.roll(gfeats[s, j], SUB - 1, 0)
            gfeats[s, rows + j] = jnp.where(
                place == SUB - 1, jnp.broadcast_to(small[j : j + 1, :], (SUB, width)), moved
            )
        total = jnp.zeros((rows, SUB, width), F32)
        for j in range(taps_len):
            total = total + taps[j, s : s + 1, :][None] * gfeats[s, j : j + rows]
        for g in lanes:
            cols = slice(g * LANES, (g + 1) * LANES)
            for r in range(rows):
                natural[2, g, pl.ds(r, SUB, stride=rows), :] = total[r, :, cols]
            outs[1 + s, :, cols] = natural[2, g, 0:length].astype(BF16)
        copy = pltpu.make_async_copy(outs.at[1 + s], (gq_out, gk_out, gv_out)[s], out_sem.at[1 + s])
        copy.start()
        out_copies.append(copy)

    for copy in ag.values():
        copy.wait_send()
    for copy in rs.values():
        copy.wait_send()
    for s in range(3):
        remote(
            (q_in, k_in, v_in)[s].at[pl.ds(length - 16, 16)], halo.at[s], h_send, h_recv, s, at_ctx(after)
        ).wait_send()
        remote(edge_send.at[s], edge_recv.at[s], e_send, e_recv, s, at_ctx(before)).wait_send()
    for way, direction in ((0, 1), (1, -1)):
        for distance in range(1, chips):
            remote(
                s_send.at[way],
                s_recv.at[way, distance],
                z_send.at[way],
                z_recv.at[way],
                distance,
                along_z(direction * distance),
            ).wait_send()
        remote(x_send.at[way], x_recv.at[way], p_send, p_recv, way, at_ctx(partner)).wait_send()
    for copy in out_copies:
        copy.wait()


def shards(query_in, key_in, value_in, short_taps, residues, decays, out_weight, out_grad):
    length, width = query_in.shape
    rows = length // SUB
    half, quarter = length // 2, length // 4
    taps_len = short_taps.shape[0]
    modes = decays.shape[1]
    chips = lax.axis_size("ctx") // 2
    vmem = pltpu.VMEM
    dma = pltpu.SemaphoreType.DMA
    scratch = [
        vmem((3, length, width), BF16),
        vmem(short_taps.shape, F32),
        vmem(residues.shape, F32),
        vmem(decays.shape, F32),
        vmem(out_weight.shape, BF16),
        vmem((SIDE, SIDE, length, width), BF16),
        vmem((3, 16, width), BF16),
        vmem((3, width // LANES, length + 8, LANES), F32),
        vmem((3, rows + 8, SUB, width), F32),
        vmem((3, rows, SUB, width), F32),
        vmem((rows, SUB, width), F32),
        vmem((2, rows, SUB, width), F32),
        vmem((rows, SUB, width), F32),
        vmem((rows, SUB, width), F32),
        vmem((rows, width), F32),
        vmem((2, modes, width), F32),
        vmem((7, modes, SUB, width), F32),
        vmem((modes, SUB, width), F32),
        vmem((modes, SUB, width), F32),
        vmem((2, modes, width), BF16),
        vmem((2, chips, modes, width), BF16),
        vmem((2, modes, width), F32),
        vmem((2, modes, width), F32),
        vmem((2, modes, width), F32),
        vmem((length, width), BF16),
        vmem((2, SIDE, half, width), F32),
        vmem((2, 2, SIDE, quarter, width), F32),
        vmem((2, SIDE, half, width), BF16),
        vmem((2, 2, SIDE, quarter, width), BF16),
        vmem((2, 2, SIDE, quarter, width), BF16),
        vmem((2, 2, SIDE, quarter, width), BF16),
        vmem((2, 2, SIDE, quarter, width), BF16),
        vmem((2, 2, SIDE, quarter, width), BF16),
        vmem((2, 4, quarter, width), BF16),
        vmem((2, 4, quarter, width), F32),
        vmem((2, 2, quarter, width), BF16),
        vmem((2, 2, quarter, width), BF16),
        vmem((2, 2, quarter, width), BF16),
        vmem((2, 2, quarter, width), BF16),
        vmem((3, rows + 8, SUB, width), F32),
        vmem((3, 16, width), BF16),
        vmem((3, 16, width), BF16),
        vmem((4, length, width), BF16),
        dma((8,)),
        dma((AG_COPIES,)),
        dma((AG_COPIES,)),
        dma((RS_COPIES,)),
        dma((RS_COPIES,)),
        dma((2, chips)),
        dma((2, chips)),
        dma((2,)),
        dma((2,)),
        dma((3,)),
        dma((3,)),
        dma((3,)),
        dma((3,)),
        dma((4,)),
    ]
    out = jax.ShapeDtypeStruct((length, width), BF16)
    return pl.pallas_call(
        functools.partial(kernel, chips, modes, taps_len),
        out_shape=(out, out, out, out),
        in_specs=[pl.BlockSpec(memory_space=pl.ANY)] * 8,
        out_specs=[pl.BlockSpec(memory_space=pl.ANY)] * 4,
        scratch_shapes=scratch,
        compiler_params=pltpu.CompilerParams(
            collective_id=0, has_side_effects=True, vmem_limit_bytes=56 * 1024 * 1024
        ),
        name="hyena",
    )(query_in, key_in, value_in, short_taps, residues, decays, out_weight, out_grad)


def solution(mesh):
    in_specs = (
        P("ctx", "ch"),
        P("ctx", "ch"),
        P("ctx", "ch"),
        P(None, None, "ch"),
        P("ch", None),
        P("ch", None),
        P("ch", None),
        P("ctx", "ch"),
    )
    out_specs = (P("ctx", "ch"), P("ctx", "ch"), P("ctx", "ch"), P("ctx", "ch"))
    return jax.shard_map(shards, mesh=mesh, in_specs=in_specs, out_specs=out_specs, check_vma=False)
```

```python
import functools

import jax
import jax.numpy as jnp
from jax import lax
from jax.experimental import pallas as pl
from jax.experimental.pallas import tpu as pltpu
from jax.sharding import PartitionSpec as P

MESH = pl.DeviceIdType.MESH
F32 = jnp.float32
BF16 = jnp.bfloat16
SIDE = 4
SUB = 8
SENDS, RECEIVES = 9, 62


def kernel(
    chips,
    modes,
    taps_len,
    q_in,
    k_in,
    v_in,
    taps_in,
    res_in,
    dec_in,
    w_in,
    g_in,
    proj_out,
    gq_out,
    gk_out,
    gv_out,
    raw,
    taps,
    res,
    dec,
    weight,
    gathered,
    halo,
    extended,
    feats,
    signal,
    conv,
    gradient,
    total_grad,
    filt,
    small,
    rates,
    decay,
    scan_buf,
    prefix,
    s_send,
    s_recv,
    x_send,
    x_recv,
    carry,
    gate,
    keep0,
    keep1,
    send_a,
    send_p,
    send_b,
    recv_a,
    recv_p,
    recv_b,
    part2,
    own2,
    send2_b,
    recv2_a,
    recv2_p,
    recv2_b,
    gfeats,
    edge_send,
    edge_recv,
    to_rows,
    to_tokens,
    local_sem,
    send_sem,
    recv_sem,
    ring_sem,
):
    length, width = q_in.shape
    rows = length // SUB
    half = length // 2
    quarter = length // 4
    ctx = lax.axis_index("ctx")
    ch = lax.axis_index("ch")
    z, core = ctx // 2, ctx % 2
    x, y = ch // SIDE, ch % SIDE
    n_ctx = 2 * chips
    before = (ctx + n_ctx - 1) % n_ctx
    after = (ctx + 1) % n_ctx
    partner = z * 2 + (1 - core)
    place = lax.broadcasted_iota(jnp.int32, (SUB, width), 0)

    def plane(axis, step):
        if axis == 0:
            other = ((x + step) % SIDE) * SIDE + y
        else:
            other = x * SIDE + (y + step) % SIDE
        return {"ctx": ctx, "ch": other}

    def along_z(step):
        return {"ctx": ((z + step) % chips) * 2 + core, "ch": ch}

    def at_ctx(other):
        return {"ctx": other, "ch": ch}

    barrier = pltpu.get_barrier_semaphore()
    peers = [plane(0, 1), plane(0, -1), plane(1, 1), plane(1, -1)]
    peers += [at_ctx(before), at_ctx(after)]
    peers += [along_z(step) for step in (1, -1, 2, -2)]
    for peer in peers:
        pl.semaphore_signal(barrier, inc=1, device_id=peer, device_id_type=MESH)

    local = [
        pltpu.make_async_copy(q_in, raw.at[0], local_sem.at[0]),
        pltpu.make_async_copy(k_in, raw.at[1], local_sem.at[1]),
        pltpu.make_async_copy(v_in, raw.at[2], local_sem.at[2]),
        pltpu.make_async_copy(dec_in, dec, local_sem.at[3]),
        pltpu.make_async_copy(res_in, res, local_sem.at[4]),
        pltpu.make_async_copy(taps_in, taps, local_sem.at[5]),
        pltpu.make_async_copy(g_in, gathered.at[0], local_sem.at[6]),
        pltpu.make_async_copy(w_in, weight, local_sem.at[7]),
    ]
    for copy in local:
        copy.start()
    pl.semaphore_wait(barrier, len(peers))

    slots, sent_on, sent = {}, {}, {}

    def slot_of(name):
        return slots.setdefault(name, len(slots))

    def send(key, group, src, dst, device):
        copy = pltpu.make_async_remote_copy(
            src_ref=src,
            dst_ref=dst,
            send_sem=send_sem.at[sent_on.setdefault(group, len(sent_on))],
            recv_sem=recv_sem.at[slot_of(key)],
            device_id=device,
            device_id_type=MESH,
        )
        sent.setdefault(key, []).append(copy)
        copy.start()

    def receive(*key, view=None):
        if view is None:
            (copy,) = sent[key]
            copy.wait_recv()
        else:
            pltpu.make_async_copy(view, view, recv_sem.at[slots[key]]).wait()

    def slot(h, i, j):
        return gathered.at[i * SIDE + j] if h == 0 else gathered.at[j * SIDE + i]

    def piece(ref, h, part):
        if part is None:
            return ref.at[pl.ds(h * half, half)]
        return ref.at[pl.ds(h * half + part * quarter, quarter)]

    def ag_copy(h, phase, source, i, j, part, step, key=None):
        axis = phase if h == 0 else 1 - phase
        send(
            ("ag", h, i, j, part, step) if key is None else key,
            "ag",
            piece(source, h, part),
            piece(slot(h, i, j), h, part),
            plane(axis, step),
        )

    def ag_wait(h, i, j, part, step):
        receive("ag", h, i, j, part, step)

    for h in range(2):
        for step in (1, -1):
            ag_copy(h, 0, g_in, step % SIDE, 0, None, step)
    for s in range(3):
        tail = (q_in, k_in, v_in)[s].at[pl.ds(length - 16, 16)]
        send(("halo",), "halo", tail, halo.at[s], at_ctx(after))
    for h in range(2):
        for step in (1, -1):
            ag_copy(h, 1, g_in, 0, step % SIDE, None, step)

    def ag_relay1():
        for h in range(2):
            for step in (1, -1):
                i = step % SIDE
                ag_wait(h, i, 0, None, step)
                ag_copy(h, 0, slot(h, i, 0), 2, 0, 0 if step == 1 else 1, step)
        for h in range(2):
            for i in (1, 3):
                for step in (1, -1):
                    ag_copy(h, 1, slot(h, i, 0), i, step % SIDE, None, step)

    def ag_relay2(i):
        for h in range(2):
            for step in (1, -1):
                j = step % SIDE
                ag_wait(h, i, j, None, step)
                ag_copy(h, 1, slot(h, i, j), i, 2, 0 if step == 1 else 1, step, ("last",))

    def ag_far():
        for h in range(2):
            for part, step in ((0, 1), (1, -1)):
                ag_wait(h, 2, 0, part, step)
                for to in (1, -1):
                    key = None if (part == 0) == (to == 1) else ("last",)
                    ag_copy(h, 1, slot(h, 2, 0), 2, to % SIDE, part, to, key)

    def ag_relay_far():
        for h in range(2):
            for step in (1, -1):
                part = 0 if step == 1 else 1
                ag_wait(h, 2, step % SIDE, part, step)
                ag_copy(h, 1, slot(h, 2, step % SIDE), 2, 2, part, step, ("last",))

    reaches = []
    while 2 * 2 ** len(reaches) < chips // 2:
        reaches.append(2 * 2 ** len(reaches))
    news = [0]

    def tell():
        if news[0] < len(reaches):
            for step in (reaches[news[0]], -reaches[news[0]]):
                pl.semaphore_signal(ring_sem.at[news[0]], inc=1, device_id=along_z(step), device_id_type=MESH)

    def pass_news():
        if news[0] < len(reaches):
            pl.semaphore_wait(ring_sem.at[news[0]], 2)
            news[0] += 1
            tell()

    tell()

    def one_hot(hit):
        return jnp.where(hit, 1.0, 0.0).astype(BF16)

    across = lax.broadcasted_iota(jnp.int32, (length, length), 1)
    down = lax.broadcasted_iota(jnp.int32, (length, length), 0)
    to_rows[...] = one_hot(across == (down % SUB) * rows + down // SUB)
    to_tokens[...] = one_hot(down == (across % SUB) * rows + across // SUB)

    def inner_order(value):
        return jnp.dot(to_rows[...], value, preferred_element_type=F32).reshape(rows, SUB, width)

    def token_order(value):
        return jnp.dot(to_tokens[...], value, preferred_element_type=F32).astype(BF16)

    local[3].wait()
    local[4].wait()
    rate = dec[...]
    rates[0] = rate
    rates[1] = res[...] * jnp.sqrt(rate)
    offsets = lax.broadcasted_iota(jnp.int32, (rows, width), 0).astype(F32)
    total = jnp.zeros((rows, width), F32)
    for n in range(modes):
        total = total + rates[1, n : n + 1, :] * jnp.exp(-rates[0, n : n + 1, :] * offsets)
    small[...] = total
    for d in range(rows):
        filt[d] = jnp.broadcast_to(small[d : d + 1, :], (SUB, width))
    for n in range(modes):
        own = jnp.broadcast_to(rates[0, n : n + 1, :], (SUB, width))
        decay[6, n] = jnp.broadcast_to(rates[1, n : n + 1, :], (SUB, width))
        decay[0, n] = jnp.exp(-own)
        step_decay = jnp.exp(-own * rows)
        decay[1, n] = step_decay
        step_decay = step_decay * step_decay
        decay[2, n] = step_decay
        step_decay = step_decay * step_decay
        decay[3, n] = step_decay
        decay[4, n] = jnp.exp(-own * (rows * place).astype(F32))
        decay[5, n] = jnp.exp(-own * (rows * (SUB - 1 - place)).astype(F32))
    block_decay = jnp.exp(-rate * length)
    pair_decay = jnp.exp(-rate * (2 * length))
    sublane = lax.broadcasted_iota(jnp.int32, (modes, SUB, width), 1)
    pass_news()

    def states(signal, direction):
        def advance(r, total):
            at = r if direction == 1 else rows - 1 - r
            return total * decay[0] + signal[at][None]

        total = lax.fori_loop(0, rows, advance, jnp.zeros((modes, SUB, width), F32))
        for level, step in enumerate((1, 2, 4)):
            if direction == 1:
                moved = jnp.where(sublane >= step, pltpu.roll(total, step, 1), 0.0)
            else:
                moved = jnp.where(sublane < SUB - step, pltpu.roll(total, SUB - step, 1), 0.0)
            total = total + decay[1 + level] * moved
        if direction == 1:
            prefix[...] = jnp.where(sublane >= 1, pltpu.roll(total, 1, 1), 0.0)
        else:
            prefix[...] = jnp.where(sublane < SUB - 1, pltpu.roll(total, SUB - 1, 1), 0.0)
        scan_buf[...] = total
        edge = SUB - 1 if direction == 1 else 0
        for n in range(modes):
            carry[0, n : n + 1, :] = scan_buf[n, edge : edge + 1, :]

    def send_states(way, direction):
        s_send[way] = carry[0].astype(BF16)
        for step in range(chips // 2, 0, -1):
            for distance in sorted({step, chips - step}):
                send(
                    ("z", way),
                    ("z", way),
                    s_send.at[way],
                    s_recv.at[way, distance - 1],
                    along_z(direction * distance),
                )

    def take_states(way, direction):
        receive("z", way, view=s_recv.at[way])
        total = jnp.zeros((modes, width), F32)
        for distance in range(chips - 1, 0, -1):
            source = z - distance if direction == 1 else chips - 1 - z - distance
            there = (source >= 0).astype(F32)
            total = total * pair_decay + there * s_recv[way, distance - 1].astype(F32)
        leads = (core == 0) if direction == 1 else (core == 1)
        leads = leads.astype(F32)
        x_send[way] = leads * (pair_decay * total + carry[0]) + (1.0 - leads) * total
        send(("x", way), ("x", way), x_send.at[way], x_recv.at[way], at_ctx(partner))
        carry[1] = block_decay * total

    def finish_states(way):
        receive("x", way)
        carry[1] = carry[1] + x_recv[way]
        for n in range(modes):
            scan_buf[n] = jnp.broadcast_to(carry[1, n : n + 1, :], (SUB, width))

    def carried_start(direction):
        reach = decay[4] if direction == 1 else decay[5]
        return decay[6] * decay[0] * (prefix[...] + reach * scan_buf[...])

    def carried(out, start, direction):
        def advance(r, state):
            at = r if direction == 1 else rows - 1 - r
            out[at] = out[at] + jnp.sum(state, axis=0)
            return state * decay[0]

        lax.fori_loop(0, rows, advance, start)

    for s in range(3):
        local[s].wait()
        extended[s, 8 : 8 + rows] = inner_order(raw[s])
    ag_relay1()
    local[5].wait()
    receive("halo", view=halo)
    first = (ctx > 0).astype(F32)
    for s in range(3):
        small[0:16] = halo[s].astype(F32) * first
        for j in range(1, taps_len):
            moved = pltpu.roll(extended[s, 8 + rows - j], 1, 0)
            extended[s, 8 - j] = jnp.where(
                place == 0, jnp.broadcast_to(small[16 - j : 17 - j, :], (SUB, width)), moved
            )
        total = jnp.zeros((rows, SUB, width), F32)
        for j in range(taps_len):
            total = total + taps[s, j : j + 1, :][None] * extended[s, 8 - j : 8 - j + rows]
        feats[s] = total
    signal[...] = (feats[1] * feats[2]).astype(BF16).astype(F32)

    states(signal, 1)
    while news[0] < len(reaches):
        pass_news()
    send_states(0, 1)
    ag_relay2(0)
    ag_far()

    conv[0] = filt[0][None] * signal[...]
    for d in range(1, rows):
        conv[0, d:rows] = conv[0, d:rows] + filt[d][None] * signal[0 : rows - d]
    ag_relay2(1)
    ag_relay2(3)

    def grad_terms(blocks):
        total = None
        for dx, dy in blocks:
            source = ((x + SIDE - dx) % SIDE) * SIDE + (y + SIDE - dy) % SIDE
            term = lax.dot_general(
                gathered[dx * SIDE + dy],
                weight[:, pl.ds(pl.multiple_of(source * width, width), width)],
                (((1,), (1,)), ((), ())),
                preferred_element_type=F32,
            )
            total = term if total is None else total + term
        return total

    local[6].wait()
    local[7].wait()
    near = [(dx, dy) for dx in (0, 1, 3) for dy in (0, 1, 3)]
    far = [(dx, dy) for dx in range(SIDE) for dy in range(SIDE) if dx == 2 or dy == 2]
    total_grad[...] = grad_terms(near)
    ag_relay_far()

    take_states(0, 1)

    receive("last", view=gathered.at[pl.ds(0, 5)])
    grad = total_grad[...] + grad_terms(far)
    high = grad.astype(BF16)
    low = (grad - high.astype(F32)).astype(BF16)
    gradient[...] = inner_order(high) + inner_order(low)
    signal[...] = (gradient[...] * feats[0]).astype(BF16).astype(F32)
    finish_states(0)
    start = carried_start(1)
    states(signal, -1)
    send_states(1, -1)

    carried(conv.at[0], start, 1)
    gate[...] = (feats[0] * conv[0]).astype(BF16).reshape(length, width)

    def rs_copy(key, src, dst, axis, step):
        send(key, "rs", src, dst, plane(axis, step))

    def first_axis(h):
        return 1 if h == 0 else 0

    lower, upper = pl.ds(0, quarter), pl.ds(quarter, quarter)

    def terms(blocks):
        for dx, dy in blocks:
            dest = ((x + dx) % SIDE) * SIDE + (y + dy) % SIDE
            product = jnp.dot(
                gate[...],
                weight[:, pl.ds(pl.multiple_of(dest * width, width), width)],
                preferred_element_type=F32,
            )
            for h in range(2):
                i, j = (dx, dy) if h == 0 else (dy, dx)
                own = product[h * half : (h + 1) * half]
                if j == 2:
                    send_a[h, i] = own.astype(BF16)
                elif j == 1:
                    keep1[h, 0, i] = own[:quarter]
                    send_p[h, 0, i] = own[quarter:].astype(BF16)
                elif j == 3:
                    keep1[h, 1, i] = own[quarter:]
                    send_p[h, 1, i] = own[:quarter].astype(BF16)
                else:
                    keep0[h, i] = own

    def a_copies(*indices):
        for i in indices:
            for h in range(2):
                rs_copy(("a", h, i, 0), send_a.at[h, i, lower], recv_a.at[h, 0, i], first_axis(h), 1)
                rs_copy(("a", h, i, 1), send_a.at[h, i, upper], recv_a.at[h, 1, i], first_axis(h), -1)

    def plain_copies(*indices, ways=(0, 1)):
        for i in indices:
            for h in range(2):
                for way in ways:
                    rs_copy(("pb", h, i), send_p.at[h, way, i], recv_p.at[h, way, i], first_axis(h), 1 - 2 * way)

    def sums_on_the_way(*indices):
        for i in indices:
            for h in range(2):
                for way in range(2):
                    receive("a", h, i, way)
                    send_b[h, way, i] = (keep1[h, way, i] + recv_a[h, way, i].astype(F32)).astype(BF16)
                    rs_copy(("pb", h, i), send_b.at[h, way, i], recv_b.at[h, way, i], first_axis(h), 1 - 2 * way)

    terms(((2, 2),))
    a_copies(2)
    terms(((2, 1), (1, 2)))
    plain_copies(2, ways=(0,))
    a_copies(1)
    terms(((2, 3), (3, 2)))
    plain_copies(2, ways=(1,))
    a_copies(3)
    terms(((1, 1), (1, 3), (3, 1), (3, 3)))
    sums_on_the_way(2)
    terms(((2, 0), (0, 2)))
    a_copies(0)
    plain_copies(1, 3)
    terms(((0, 1), (1, 0), (0, 3), (3, 0), (0, 0)))
    sums_on_the_way(1, 3)
    plain_copies(0)
    sums_on_the_way(0)

    def edges(s, key):
        for j in range(16):
            small[j : j + 1, :] = gfeats[s, j, 0:1, :]
        edge_send[s] = small[0:16].astype(BF16)
        send(key, key, edge_send.at[s], edge_recv.at[s], at_ctx(before))

    gfeats[0, 0:rows] = (gradient[...] * conv[0]).astype(BF16).astype(F32)
    edges(0, ("edge", 0))
    conv[1] = filt[0][None] * signal[...]
    for d in range(1, rows):
        conv[1, 0 : rows - d] = conv[1, 0 : rows - d] + filt[d][None] * signal[d:rows]

    def collect(h, i):
        receive("pb", h, i, view=send_a.at[h, pl.ds(0, 2)])
        low = keep0[h, i, 0:quarter] + recv_b[h, 0, i].astype(F32) + recv_p[h, 1, i].astype(F32)
        high = keep0[h, i, quarter:half] + recv_p[h, 0, i].astype(F32) + recv_b[h, 1, i].astype(F32)
        return low, high

    for h in range(2):
        axis = 1 - first_axis(h)
        low, high = collect(h, 2)
        part2[h, 0] = low.astype(BF16)
        part2[h, 1] = high.astype(BF16)
        rs_copy(("a2", h, 0), part2.at[h, 0], recv2_a.at[h, 0], axis, 1)
        rs_copy(("a2", h, 1), part2.at[h, 1], recv2_a.at[h, 1], axis, -1)

    last = (ctx < n_ctx - 1).astype(F32)

    def featurize_back(s):
        small[0:16] = edge_recv[s].astype(F32) * last
        for j in range(taps_len - 1):
            moved = pltpu.roll(gfeats[s, j], SUB - 1, 0)
            gfeats[s, rows + j] = jnp.where(
                place == SUB - 1, jnp.broadcast_to(small[j : j + 1, :], (SUB, width)), moved
            )
        total = jnp.zeros((rows, SUB, width), F32)
        for j in range(taps_len):
            total = total + taps[s, j : j + 1, :][None] * gfeats[s, j : j + rows]
        (gq_out, gk_out, gv_out)[s][...] = token_order(total.astype(BF16).reshape(length, width))

    take_states(1, -1)
    receive("edge", 0)
    featurize_back(0)
    finish_states(1)
    carried(conv.at[1], carried_start(-1), -1)
    gfeats[1, 0:rows] = (conv[1] * feats[2]).astype(BF16).astype(F32)
    edges(1, ("edge", 1))
    gfeats[2, 0:rows] = (conv[1] * feats[1]).astype(BF16).astype(F32)
    edges(2, ("edge", 1))

    for h in range(2):
        axis = 1 - first_axis(h)
        low, high = collect(h, 1)
        own2[h, 0] = low
        part2[h, 2] = high.astype(BF16)
        rs_copy(("pb2", h), part2.at[h, 2], recv2_p.at[h, 0], axis, 1)
        low, high = collect(h, 3)
        own2[h, 1] = high
        part2[h, 3] = low.astype(BF16)
        rs_copy(("pb2", h), part2.at[h, 3], recv2_p.at[h, 1], axis, -1)
        for way in range(2):
            receive("a2", h, way)
            send2_b[h, way] = (own2[h, way] + recv2_a[h, way].astype(F32)).astype(BF16)
            rs_copy(("pb2", h), send2_b.at[h, way], recv2_b.at[h, way], axis, 1 - 2 * way)
    for h in range(2):
        low, high = collect(h, 0)
        own2[h, 2] = low
        own2[h, 3] = high

    receive("edge", 1, view=edge_recv.at[pl.ds(0, 2)])
    featurize_back(1)
    featurize_back(2)

    for h in range(2):
        receive("pb2", h, view=send_a.at[h, pl.ds(0, 2)])
        low = own2[h, 2] + recv2_b[h, 0].astype(F32) + recv2_p[h, 1].astype(F32)
        high = own2[h, 3] + recv2_p[h, 0].astype(F32) + recv2_b[h, 1].astype(F32)
        gate[h * half : h * half + quarter] = low.astype(BF16)
        gate[h * half + quarter : (h + 1) * half] = high.astype(BF16)
    proj_out[...] = token_order(gate[...])

    views = {
        "ag": gathered.at[pl.ds(0, SIDE * SIDE - 1)],
        "rs": gathered.at[pl.ds(0, SIDE * SIDE - 1)],
        "halo": halo,
        ("z", 0): s_recv.at[0],
        ("z", 1): s_recv.at[1],
        ("x", 0): x_recv.at[0],
        ("x", 1): x_recv.at[1],
        ("edge", 0): edge_recv.at[0],
        ("edge", 1): edge_recv.at[pl.ds(0, 2)],
    }
    assert (len(sent_on), len(slots)) == (SENDS, RECEIVES)
    for group, index in sent_on.items():
        pltpu.make_async_copy(views[group], views[group], send_sem.at[index]).wait()


def deliver(*refs):
    sources, targets, sem = refs[:4], refs[4:8], refs[8]
    copies = [pltpu.make_async_copy(sources[i], targets[i], sem.at[i]) for i in range(4)]
    for copy in copies:
        copy.start()
    for copy in copies:
        copy.wait()


def shards(query_in, key_in, value_in, short_taps, residues, decays, out_weight, out_grad):
    length, width = query_in.shape
    rows = length // SUB
    half, quarter = length // 2, length // 4
    short_taps = jnp.transpose(short_taps, (1, 0, 2))
    residues, decays = residues.T, decays.T
    taps_len = short_taps.shape[1]
    modes = decays.shape[0]
    chips = lax.axis_size("ctx") // 2
    vmem = pltpu.VMEM
    dma = pltpu.SemaphoreType.DMA
    scratch = [
        vmem((3, length, width), BF16),
        vmem(short_taps.shape, F32),
        vmem(residues.shape, F32),
        vmem(decays.shape, F32),
        vmem(out_weight.shape, BF16),
        vmem((SIDE * SIDE, length, width), BF16),
        vmem((3, 16, width), BF16),
        vmem((3, rows + 8, SUB, width), F32),
        vmem((3, rows, SUB, width), F32),
        vmem((rows, SUB, width), F32),
        vmem((2, rows, SUB, width), F32),
        vmem((rows, SUB, width), F32),
        vmem((length, width), F32),
        vmem((rows, SUB, width), F32),
        vmem((rows, width), F32),
        vmem((2, modes, width), F32),
        vmem((7, modes, SUB, width), F32),
        vmem((modes, SUB, width), F32),
        vmem((modes, SUB, width), F32),
        vmem((2, modes, width), BF16),
        vmem((2, chips - 1, modes, width), BF16),
        vmem((2, modes, width), F32),
        vmem((2, modes, width), F32),
        vmem((2, modes, width), F32),
        vmem((length, width), BF16),
        vmem((2, SIDE, half, width), F32),
        vmem((2, 2, SIDE, quarter, width), F32),
        vmem((2, SIDE, half, width), BF16),
        vmem((2, 2, SIDE, quarter, width), BF16),
        vmem((2, 2, SIDE, quarter, width), BF16),
        vmem((2, 2, SIDE, quarter, width), BF16),
        vmem((2, 2, SIDE, quarter, width), BF16),
        vmem((2, 2, SIDE, quarter, width), BF16),
        vmem((2, 4, quarter, width), BF16),
        vmem((2, 4, quarter, width), F32),
        vmem((2, 2, quarter, width), BF16),
        vmem((2, 2, quarter, width), BF16),
        vmem((2, 2, quarter, width), BF16),
        vmem((2, 2, quarter, width), BF16),
        vmem((3, rows + 8, SUB, width), F32),
        vmem((3, 16, width), BF16),
        vmem((3, 16, width), BF16),
        vmem((length, length), BF16),
        vmem((length, length), BF16),
        dma((8,)),
        dma((SENDS,)),
        dma((RECEIVES,)),
        pltpu.SemaphoreType.REGULAR((2,)),
    ]
    out = jax.ShapeDtypeStruct((length, width), BF16)
    results = pl.pallas_call(
        functools.partial(kernel, chips, modes, taps_len),
        out_shape=(out, out, out, out),
        in_specs=[pl.BlockSpec(memory_space=pl.ANY)] * 8,
        out_specs=[pl.BlockSpec(memory_space=pltpu.VMEM)] * 4,
        scratch_shapes=scratch,
        compiler_params=pltpu.CompilerParams(
            collective_id=0, has_side_effects=True, vmem_limit_bytes=56 * 1024 * 1024
        ),
        name="hyena",
    )(query_in, key_in, value_in, short_taps, residues, decays, out_weight, out_grad)
    return pl.pallas_call(
        deliver,
        out_shape=(out, out, out, out),
        in_specs=[pl.BlockSpec(memory_space=pltpu.VMEM)] * 4,
        out_specs=[pl.BlockSpec(memory_space=pl.ANY)] * 4,
        scratch_shapes=[dma((4,))],
        name="deliver",
    )(*results)


def solution(mesh):
    in_specs = (
        P("ctx", "ch"),
        P("ctx", "ch"),
        P("ctx", "ch"),
        P(None, None, "ch"),
        P("ch", None),
        P("ch", None),
        P("ch", None),
        P("ctx", "ch"),
    )
    out_specs = (P("ctx", "ch"), P("ctx", "ch"), P("ctx", "ch"), P("ctx", "ch"))
    return jax.shard_map(shards, mesh=mesh, in_specs=in_specs, out_specs=out_specs, check_vma=False)
```

```python
import functools

import jax
import jax.numpy as jnp
from jax import lax
from jax.experimental import pallas as pl
from jax.experimental.pallas import tpu as pltpu
from jax.sharding import PartitionSpec as P

MESH = pl.DeviceIdType.MESH
F32 = jnp.float32
BF16 = jnp.bfloat16
SIDE = 4
SUB = 8
LANES = 128
UNROLL = 2
SENDS, RECEIVES = 9, 62


def kernel(
    chips,
    modes,
    taps_len,
    q_in,
    k_in,
    v_in,
    taps_in,
    res_in,
    dec_in,
    w_in,
    g_in,
    proj_out,
    gq_out,
    gk_out,
    gv_out,
    raw,
    taps,
    res,
    dec,
    weight,
    gathered,
    halo,
    extended,
    feats,
    signal,
    conv,
    gradient,
    total_grad,
    filt,
    small,
    rates,
    decay,
    scan_buf,
    prefix,
    s_send,
    s_recv,
    x_send,
    x_recv,
    carry,
    gate,
    keep0,
    keep1,
    send_a,
    send_p,
    send_b,
    recv_a,
    recv_p,
    recv_b,
    part2,
    own2,
    send2_b,
    recv2_a,
    recv2_p,
    recv2_b,
    gfeats,
    edge_send,
    edge_recv,
    to_rows,
    to_tokens,
    local_sem,
    send_sem,
    recv_sem,
    ring_sem,
):
    length, width = q_in.shape
    rows = length // SUB
    half = length // 2
    quarter = length // 4
    ctx = lax.axis_index("ctx")
    ch = lax.axis_index("ch")
    z, core = ctx // 2, ctx % 2
    x, y = ch // SIDE, ch % SIDE
    n_ctx = 2 * chips
    before = (ctx + n_ctx - 1) % n_ctx
    after = (ctx + 1) % n_ctx
    partner = z * 2 + (1 - core)
    place = lax.broadcasted_iota(jnp.int32, (SUB, width), 0)

    def plane(axis, step):
        if axis == 0:
            other = ((x + step) % SIDE) * SIDE + y
        else:
            other = x * SIDE + (y + step) % SIDE
        return {"ctx": ctx, "ch": other}

    def along_z(step):
        return {"ctx": ((z + step) % chips) * 2 + core, "ch": ch}

    def at_ctx(other):
        return {"ctx": other, "ch": ch}

    barrier = pltpu.get_barrier_semaphore()
    peers = [plane(0, 1), plane(0, -1), plane(1, 1), plane(1, -1)]
    peers += [at_ctx(before), at_ctx(after)]
    peers += [along_z(step) for step in (1, -1, 2, -2)]
    for peer in peers:
        pl.semaphore_signal(barrier, inc=1, device_id=peer, device_id_type=MESH)

    local = [
        pltpu.make_async_copy(q_in, raw.at[0], local_sem.at[0]),
        pltpu.make_async_copy(k_in, raw.at[1], local_sem.at[1]),
        pltpu.make_async_copy(v_in, raw.at[2], local_sem.at[2]),
        pltpu.make_async_copy(dec_in, dec, local_sem.at[3]),
        pltpu.make_async_copy(res_in, res, local_sem.at[4]),
        pltpu.make_async_copy(taps_in, taps, local_sem.at[5]),
        pltpu.make_async_copy(g_in, gathered.at[0], local_sem.at[6]),
        pltpu.make_async_copy(w_in, weight, local_sem.at[7]),
    ]
    for copy in local:
        copy.start()
    pl.semaphore_wait(barrier, len(peers))

    slots, sent_on, sent = {}, {}, {}

    def slot_of(name):
        return slots.setdefault(name, len(slots))

    def send(key, group, src, dst, device):
        copy = pltpu.make_async_remote_copy(
            src_ref=src,
            dst_ref=dst,
            send_sem=send_sem.at[sent_on.setdefault(group, len(sent_on))],
            recv_sem=recv_sem.at[slot_of(key)],
            device_id=device,
            device_id_type=MESH,
        )
        sent.setdefault(key, []).append(copy)
        copy.start()

    def receive(*key, view=None):
        if view is None:
            (copy,) = sent[key]
            copy.wait_recv()
        else:
            pltpu.make_async_copy(view, view, recv_sem.at[slots[key]]).wait()

    def slot(h, i, j):
        return gathered.at[i * SIDE + j] if h == 0 else gathered.at[j * SIDE + i]

    def piece(ref, h, part):
        if part is None:
            return ref.at[pl.ds(h * half, half)]
        return ref.at[pl.ds(h * half + part * quarter, quarter)]

    def ag_copy(h, phase, source, i, j, part, step, key=None):
        axis = phase if h == 0 else 1 - phase
        send(
            ("ag", h, i, j, part, step) if key is None else key,
            "ag",
            piece(source, h, part),
            piece(slot(h, i, j), h, part),
            plane(axis, step),
        )

    def ag_wait(h, i, j, part, step):
        receive("ag", h, i, j, part, step)

    for h in range(2):
        for step in (1, -1):
            ag_copy(h, 0, g_in, step % SIDE, 0, None, step)
    for s in range(3):
        tail = (q_in, k_in, v_in)[s].at[pl.ds(length - 16, 16)]
        send(("halo",), "halo", tail, halo.at[s], at_ctx(after))
    for h in range(2):
        for step in (1, -1):
            ag_copy(h, 1, g_in, 0, step % SIDE, None, step)

    def ag_relay1():
        for h in range(2):
            for step in (1, -1):
                i = step % SIDE
                ag_wait(h, i, 0, None, step)
                ag_copy(h, 0, slot(h, i, 0), 2, 0, 0 if step == 1 else 1, step)
        for h in range(2):
            for i in (1, 3):
                for step in (1, -1):
                    ag_copy(h, 1, slot(h, i, 0), i, step % SIDE, None, step)

    def ag_relay2(i):
        for h in range(2):
            for step in (1, -1):
                j = step % SIDE
                ag_wait(h, i, j, None, step)
                ag_copy(h, 1, slot(h, i, j), i, 2, 0 if step == 1 else 1, step, ("last",))

    def ag_far():
        for h in range(2):
            for part, step in ((0, 1), (1, -1)):
                ag_wait(h, 2, 0, part, step)
                for to in (1, -1):
                    key = None if (part == 0) == (to == 1) else ("last",)
                    ag_copy(h, 1, slot(h, 2, 0), 2, to % SIDE, part, to, key)

    def ag_relay_far():
        for h in range(2):
            for step in (1, -1):
                part = 0 if step == 1 else 1
                ag_wait(h, 2, step % SIDE, part, step)
                ag_copy(h, 1, slot(h, 2, step % SIDE), 2, 2, part, step, ("last",))

    reaches = []
    while 2 * 2 ** len(reaches) < chips // 2:
        reaches.append(2 * 2 ** len(reaches))
    news = [0]

    def tell():
        if news[0] < len(reaches):
            for step in (reaches[news[0]], -reaches[news[0]]):
                pl.semaphore_signal(ring_sem.at[news[0]], inc=1, device_id=along_z(step), device_id_type=MESH)

    def pass_news():
        if news[0] < len(reaches):
            pl.semaphore_wait(ring_sem.at[news[0]], 2)
            news[0] += 1
            tell()

    tell()

    def one_hot(hit):
        return jnp.where(hit, 1.0, 0.0).astype(BF16)

    across = lax.broadcasted_iota(jnp.int32, (length, length), 1)
    down = lax.broadcasted_iota(jnp.int32, (length, length), 0)
    to_rows[...] = one_hot(across == (down % SUB) * rows + down // SUB)
    to_tokens[...] = one_hot(down == (across % SUB) * rows + across // SUB)

    def inner_order(value):
        return jnp.dot(to_rows[...], value, preferred_element_type=F32).reshape(rows, SUB, width)

    def token_order(value):
        return jnp.dot(to_tokens[...], value, preferred_element_type=F32).astype(BF16)

    local[3].wait()
    local[4].wait()
    rate = dec[...]
    rates[0] = rate
    rates[1] = res[...] * jnp.sqrt(rate)
    offsets = lax.broadcasted_iota(jnp.int32, (rows, width), 0).astype(F32)
    total = jnp.zeros((rows, width), F32)
    for n in range(modes):
        total = total + rates[1, n : n + 1, :] * jnp.exp(-rates[0, n : n + 1, :] * offsets)
    small[...] = total
    for d in range(rows):
        filt[d] = jnp.broadcast_to(small[d : d + 1, :], (SUB, width))
    for n in range(modes):
        own = jnp.broadcast_to(rates[0, n : n + 1, :], (SUB, width))
        decay[6, n] = jnp.broadcast_to(rates[1, n : n + 1, :], (SUB, width))
        decay[0, n] = jnp.exp(-own)
        step_decay = jnp.exp(-own * rows)
        decay[1, n] = step_decay
        step_decay = step_decay * step_decay
        decay[2, n] = step_decay
        step_decay = step_decay * step_decay
        decay[3, n] = step_decay
        decay[4, n] = jnp.exp(-own * (rows * place).astype(F32))
        decay[5, n] = jnp.exp(-own * (rows * (SUB - 1 - place)).astype(F32))
    block_decay = jnp.exp(-rate * length)
    pair_decay = jnp.exp(-rate * (2 * length))
    sublane = lax.broadcasted_iota(jnp.int32, (modes, SUB, width), 1)
    pass_news()

    def states(signal, direction):
        for lo in range(0, width, LANES):
            cols = slice(lo, lo + LANES)
            step_decay = decay[0, :, :, cols]

            def advance(r, total):
                for k in range(UNROLL):
                    at = UNROLL * r + k if direction == 1 else rows - 1 - k - UNROLL * r
                    total = total * step_decay + signal[at, :, cols][None]
                return total

            scan_buf[:, :, cols] = lax.fori_loop(0, rows // UNROLL, advance, jnp.zeros((modes, SUB, LANES), F32))
        total = scan_buf[...]
        for level, step in enumerate((1, 2, 4)):
            if direction == 1:
                moved = jnp.where(sublane >= step, pltpu.roll(total, step, 1), 0.0)
            else:
                moved = jnp.where(sublane < SUB - step, pltpu.roll(total, SUB - step, 1), 0.0)
            total = total + decay[1 + level] * moved
        if direction == 1:
            prefix[...] = jnp.where(sublane >= 1, pltpu.roll(total, 1, 1), 0.0)
        else:
            prefix[...] = jnp.where(sublane < SUB - 1, pltpu.roll(total, SUB - 1, 1), 0.0)
        scan_buf[...] = total
        edge = SUB - 1 if direction == 1 else 0
        for n in range(modes):
            carry[0, n : n + 1, :] = scan_buf[n, edge : edge + 1, :]

    def send_states(way, direction):
        s_send[way] = carry[0].astype(BF16)
        for step in range(chips // 2, 0, -1):
            for distance in sorted({step, chips - step}):
                send(
                    ("z", way),
                    ("z", way),
                    s_send.at[way],
                    s_recv.at[way, distance - 1],
                    along_z(direction * distance),
                )

    def take_states(way, direction):
        receive("z", way, view=s_recv.at[way])
        total = jnp.zeros((modes, width), F32)
        for distance in range(chips - 1, 0, -1):
            source = z - distance if direction == 1 else chips - 1 - z - distance
            there = (source >= 0).astype(F32)
            total = total * pair_decay + there * s_recv[way, distance - 1].astype(F32)
        leads = (core == 0) if direction == 1 else (core == 1)
        leads = leads.astype(F32)
        x_send[way] = leads * (pair_decay * total + carry[0]) + (1.0 - leads) * total
        send(("x", way), ("x", way), x_send.at[way], x_recv.at[way], at_ctx(partner))
        carry[1] = block_decay * total

    def finish_states(way):
        receive("x", way)
        carry[1] = carry[1] + x_recv[way]
        for n in range(modes):
            scan_buf[n] = jnp.broadcast_to(carry[1, n : n + 1, :], (SUB, width))

    def carried_start(direction):
        reach = decay[4] if direction == 1 else decay[5]
        return decay[6] * decay[0] * (prefix[...] + reach * scan_buf[...])

    def carried(out, start, direction):
        for lo in range(0, width, LANES):
            cols = slice(lo, lo + LANES)
            step_decay = decay[0, :, :, cols]

            def advance(r, state):
                for k in range(UNROLL):
                    at = UNROLL * r + k if direction == 1 else rows - 1 - k - UNROLL * r
                    out[at, :, cols] = out[at, :, cols] + jnp.sum(state, axis=0)
                    state = state * step_decay
                return state

            lax.fori_loop(0, rows // UNROLL, advance, start[:, :, cols])

    for s in range(3):
        local[s].wait()
        extended[s, 8 : 8 + rows] = inner_order(raw[s])
    ag_relay1()
    local[5].wait()
    receive("halo", view=halo)
    first = (ctx > 0).astype(F32)
    for s in range(3):
        small[0:16] = halo[s].astype(F32) * first
        for j in range(1, taps_len):
            moved = pltpu.roll(extended[s, 8 + rows - j], 1, 0)
            extended[s, 8 - j] = jnp.where(
                place == 0, jnp.broadcast_to(small[16 - j : 17 - j, :], (SUB, width)), moved
            )
        total = jnp.zeros((rows, SUB, width), F32)
        for j in range(taps_len):
            total = total + taps[s, j : j + 1, :][None] * extended[s, 8 - j : 8 - j + rows]
        feats[s] = total
    signal[...] = (feats[1] * feats[2]).astype(BF16).astype(F32)

    states(signal, 1)
    while news[0] < len(reaches):
        pass_news()
    send_states(0, 1)
    ag_far()
    ag_relay2(0)

    conv[0] = filt[0][None] * signal[...]
    for d in range(1, rows):
        conv[0, d:rows] = conv[0, d:rows] + filt[d][None] * signal[0 : rows - d]
    ag_relay2(1)
    ag_relay2(3)
    ag_relay_far()

    def grad_terms(blocks):
        total = None
        for dx, dy in blocks:
            source = ((x + SIDE - dx) % SIDE) * SIDE + (y + SIDE - dy) % SIDE
            term = lax.dot_general(
                gathered[dx * SIDE + dy],
                weight[:, pl.ds(pl.multiple_of(source * width, width), width)],
                (((1,), (1,)), ((), ())),
                preferred_element_type=F32,
            )
            total = term if total is None else total + term
        return total

    local[6].wait()
    local[7].wait()
    near = [(dx, dy) for dx in (0, 1, 3) for dy in (0, 1, 3)]
    far = [(dx, dy) for dx in range(SIDE) for dy in range(SIDE) if dx == 2 or dy == 2]
    total_grad[...] = grad_terms(near)

    take_states(0, 1)

    receive("last", view=gathered.at[pl.ds(0, 5)])
    grad = total_grad[...] + grad_terms(far)
    high = grad.astype(BF16)
    low = (grad - high.astype(F32)).astype(BF16)
    gradient[...] = inner_order(high) + inner_order(low)
    signal[...] = (gradient[...] * feats[0]).astype(BF16).astype(F32)
    finish_states(0)

    carried(conv.at[0], carried_start(1), 1)
    gate[...] = (feats[0] * conv[0]).astype(BF16).reshape(length, width)

    def rs_copy(key, src, dst, axis, step):
        send(key, "rs", src, dst, plane(axis, step))

    def first_axis(h):
        return 1 if h == 0 else 0

    lower, upper = pl.ds(0, quarter), pl.ds(quarter, quarter)

    def terms(blocks):
        for dx, dy in blocks:
            dest = ((x + dx) % SIDE) * SIDE + (y + dy) % SIDE
            product = jnp.dot(
                gate[...],
                weight[:, pl.ds(pl.multiple_of(dest * width, width), width)],
                preferred_element_type=F32,
            )
            for h in range(2):
                i, j = (dx, dy) if h == 0 else (dy, dx)
                own = product[h * half : (h + 1) * half]
                if j == 2:
                    send_a[h, i] = own.astype(BF16)
                elif j == 1:
                    keep1[h, 0, i] = own[:quarter]
                    send_p[h, 0, i] = own[quarter:].astype(BF16)
                elif j == 3:
                    keep1[h, 1, i] = own[quarter:]
                    send_p[h, 1, i] = own[:quarter].astype(BF16)
                else:
                    keep0[h, i] = own

    def a_copies(*indices):
        for i in indices:
            for h in range(2):
                rs_copy(("a", h, i, 0), send_a.at[h, i, lower], recv_a.at[h, 0, i], first_axis(h), 1)
                rs_copy(("a", h, i, 1), send_a.at[h, i, upper], recv_a.at[h, 1, i], first_axis(h), -1)

    def plain_copies(*indices, ways=(0, 1)):
        for i in indices:
            for h in range(2):
                for way in ways:
                    rs_copy(("pb", h, i), send_p.at[h, way, i], recv_p.at[h, way, i], first_axis(h), 1 - 2 * way)

    def sums_on_the_way(*indices):
        for i in indices:
            for h in range(2):
                for way in range(2):
                    receive("a", h, i, way)
                    send_b[h, way, i] = (keep1[h, way, i] + recv_a[h, way, i].astype(F32)).astype(BF16)
                    rs_copy(("pb", h, i), send_b.at[h, way, i], recv_b.at[h, way, i], first_axis(h), 1 - 2 * way)

    terms(((2, 2),))
    a_copies(2)
    terms(((2, 1), (1, 2)))
    plain_copies(2, ways=(0,))
    a_copies(1)

    states(signal, -1)
    send_states(1, -1)

    terms(((2, 3), (3, 2)))
    plain_copies(2, ways=(1,))
    a_copies(3)
    terms(((1, 1), (1, 3), (3, 1), (3, 3)))
    plain_copies(1, 3)
    sums_on_the_way(2)
    sums_on_the_way(1, 3)
    terms(((2, 0), (0, 2)))
    a_copies(0)
    terms(((0, 1), (1, 0), (0, 3), (3, 0), (0, 0)))
    plain_copies(0)

    def edges(s, key):
        for j in range(16):
            small[j : j + 1, :] = gfeats[s, j, 0:1, :]
        edge_send[s] = small[0:16].astype(BF16)
        send(key, key, edge_send.at[s], edge_recv.at[s], at_ctx(before))

    gfeats[0, 0:rows] = (gradient[...] * conv[0]).astype(BF16).astype(F32)
    edges(0, ("edge", 0))
    conv[1] = filt[0][None] * signal[...]
    for d in range(1, rows):
        conv[1, 0 : rows - d] = conv[1, 0 : rows - d] + filt[d][None] * signal[d:rows]

    def collect(h, i):
        receive("pb", h, i, view=send_a.at[h, pl.ds(0, 2)])
        low = keep0[h, i, 0:quarter] + recv_b[h, 0, i].astype(F32) + recv_p[h, 1, i].astype(F32)
        high = keep0[h, i, quarter:half] + recv_p[h, 0, i].astype(F32) + recv_b[h, 1, i].astype(F32)
        return low, high

    for h in range(2):
        axis = 1 - first_axis(h)
        low, high = collect(h, 2)
        part2[h, 0] = low.astype(BF16)
        part2[h, 1] = high.astype(BF16)
        rs_copy(("a2", h, 0), part2.at[h, 0], recv2_a.at[h, 0], axis, 1)
        rs_copy(("a2", h, 1), part2.at[h, 1], recv2_a.at[h, 1], axis, -1)
    sums_on_the_way(0)

    last = (ctx < n_ctx - 1).astype(F32)

    def featurize_back(s):
        small[0:16] = edge_recv[s].astype(F32) * last
        for j in range(taps_len - 1):
            moved = pltpu.roll(gfeats[s, j], SUB - 1, 0)
            gfeats[s, rows + j] = jnp.where(
                place == SUB - 1, jnp.broadcast_to(small[j : j + 1, :], (SUB, width)), moved
            )
        total = jnp.zeros((rows, SUB, width), F32)
        for j in range(taps_len):
            total = total + taps[s, j : j + 1, :][None] * gfeats[s, j : j + rows]
        (gq_out, gk_out, gv_out)[s][...] = token_order(total.astype(BF16).reshape(length, width))

    take_states(1, -1)

    for h in range(2):
        axis = 1 - first_axis(h)
        low, high = collect(h, 1)
        own2[h, 0] = low
        part2[h, 2] = high.astype(BF16)
        rs_copy(("pb2", h), part2.at[h, 2], recv2_p.at[h, 0], axis, 1)
        low, high = collect(h, 3)
        own2[h, 1] = high
        part2[h, 3] = low.astype(BF16)
        rs_copy(("pb2", h), part2.at[h, 3], recv2_p.at[h, 1], axis, -1)
        for way in range(2):
            receive("a2", h, way)
            send2_b[h, way] = (own2[h, way] + recv2_a[h, way].astype(F32)).astype(BF16)
            rs_copy(("pb2", h), send2_b.at[h, way], recv2_b.at[h, way], axis, 1 - 2 * way)

    finish_states(1)
    carried(conv.at[1], carried_start(-1), -1)
    gfeats[1, 0:rows] = (conv[1] * feats[2]).astype(BF16).astype(F32)
    edges(1, ("edge", 1))
    gfeats[2, 0:rows] = (conv[1] * feats[1]).astype(BF16).astype(F32)
    edges(2, ("edge", 1))
    receive("edge", 0)
    featurize_back(0)
    for h in range(2):
        low, high = collect(h, 0)
        own2[h, 2] = low
        own2[h, 3] = high

    receive("edge", 1, view=edge_recv.at[pl.ds(0, 2)])
    featurize_back(1)
    featurize_back(2)

    for h in range(2):
        receive("pb2", h, view=send_a.at[h, pl.ds(0, 2)])
        low = own2[h, 2] + recv2_b[h, 0].astype(F32) + recv2_p[h, 1].astype(F32)
        high = own2[h, 3] + recv2_p[h, 0].astype(F32) + recv2_b[h, 1].astype(F32)
        gate[h * half : h * half + quarter] = low.astype(BF16)
        gate[h * half + quarter : (h + 1) * half] = high.astype(BF16)
    proj_out[...] = token_order(gate[...])

    views = {
        "ag": gathered.at[pl.ds(0, SIDE * SIDE - 1)],
        "rs": gathered.at[pl.ds(0, SIDE * SIDE - 1)],
        "halo": halo,
        ("z", 0): s_recv.at[0],
        ("z", 1): s_recv.at[1],
        ("x", 0): x_recv.at[0],
        ("x", 1): x_recv.at[1],
        ("edge", 0): edge_recv.at[0],
        ("edge", 1): edge_recv.at[pl.ds(0, 2)],
    }
    assert (len(sent_on), len(slots)) == (SENDS, RECEIVES)
    for group, index in sent_on.items():
        pltpu.make_async_copy(views[group], views[group], send_sem.at[index]).wait()


def deliver(*refs):
    sources, targets, sem = refs[:4], refs[4:8], refs[8]
    copies = [pltpu.make_async_copy(sources[i], targets[i], sem.at[i]) for i in range(4)]
    for copy in copies:
        copy.start()
    for copy in copies:
        copy.wait()


def shards(query_in, key_in, value_in, short_taps, residues, decays, out_weight, out_grad):
    length, width = query_in.shape
    rows = length // SUB
    half, quarter = length // 2, length // 4
    short_taps = jnp.transpose(short_taps, (1, 0, 2))
    residues, decays = residues.T, decays.T
    taps_len = short_taps.shape[1]
    modes = decays.shape[0]
    chips = lax.axis_size("ctx") // 2
    vmem = pltpu.VMEM
    dma = pltpu.SemaphoreType.DMA
    scratch = [
        vmem((3, length, width), BF16),
        vmem(short_taps.shape, F32),
        vmem(residues.shape, F32),
        vmem(decays.shape, F32),
        vmem(out_weight.shape, BF16),
        vmem((SIDE * SIDE, length, width), BF16),
        vmem((3, 16, width), BF16),
        vmem((3, rows + 8, SUB, width), F32),
        vmem((3, rows, SUB, width), F32),
        vmem((rows, SUB, width), F32),
        vmem((2, rows, SUB, width), F32),
        vmem((rows, SUB, width), F32),
        vmem((length, width), F32),
        vmem((rows, SUB, width), F32),
        vmem((rows, width), F32),
        vmem((2, modes, width), F32),
        vmem((7, modes, SUB, width), F32),
        vmem((modes, SUB, width), F32),
        vmem((modes, SUB, width), F32),
        vmem((2, modes, width), BF16),
        vmem((2, chips - 1, modes, width), BF16),
        vmem((2, modes, width), F32),
        vmem((2, modes, width), F32),
        vmem((2, modes, width), F32),
        vmem((length, width), BF16),
        vmem((2, SIDE, half, width), F32),
        vmem((2, 2, SIDE, quarter, width), F32),
        vmem((2, SIDE, half, width), BF16),
        vmem((2, 2, SIDE, quarter, width), BF16),
        vmem((2, 2, SIDE, quarter, width), BF16),
        vmem((2, 2, SIDE, quarter, width), BF16),
        vmem((2, 2, SIDE, quarter, width), BF16),
        vmem((2, 2, SIDE, quarter, width), BF16),
        vmem((2, 4, quarter, width), BF16),
        vmem((2, 4, quarter, width), F32),
        vmem((2, 2, quarter, width), BF16),
        vmem((2, 2, quarter, width), BF16),
        vmem((2, 2, quarter, width), BF16),
        vmem((2, 2, quarter, width), BF16),
        vmem((3, rows + 8, SUB, width), F32),
        vmem((3, 16, width), BF16),
        vmem((3, 16, width), BF16),
        vmem((length, length), BF16),
        vmem((length, length), BF16),
        dma((8,)),
        dma((SENDS,)),
        dma((RECEIVES,)),
        pltpu.SemaphoreType.REGULAR((2,)),
    ]
    out = jax.ShapeDtypeStruct((length, width), BF16)
    results = pl.pallas_call(
        functools.partial(kernel, chips, modes, taps_len),
        out_shape=(pltpu.VMEM((length, width), BF16),) * 4,
        in_specs=[pl.BlockSpec(memory_space=pl.ANY)] * 8,
        out_specs=[pl.BlockSpec(memory_space=pltpu.VMEM)] * 4,
        scratch_shapes=scratch,
        compiler_params=pltpu.CompilerParams(
            collective_id=0, has_side_effects=True, vmem_limit_bytes=56 * 1024 * 1024
        ),
        name="hyena",
    )(query_in, key_in, value_in, short_taps, residues, decays, out_weight, out_grad)
    return pl.pallas_call(
        deliver,
        out_shape=(out, out, out, out),
        in_specs=[pl.BlockSpec(memory_space=pltpu.VMEM)] * 4,
        out_specs=[pl.BlockSpec(memory_space=pl.ANY)] * 4,
        scratch_shapes=[dma((4,))],
        name="deliver",
    )(*[pltpu.with_memory_space_constraint(r, pltpu.VMEM) for r in results])


def solution(mesh):
    in_specs = (
        P("ctx", "ch"),
        P("ctx", "ch"),
        P("ctx", "ch"),
        P(None, None, "ch"),
        P("ch", None),
        P("ch", None),
        P("ch", None),
        P("ctx", "ch"),
    )
    out_specs = (P("ctx", "ch"), P("ctx", "ch"), P("ctx", "ch"), P("ctx", "ch"))
    return jax.shard_map(shards, mesh=mesh, in_specs=in_specs, out_specs=out_specs, check_vma=False)
```

```python
import functools

import jax
import jax.numpy as jnp
from jax import lax
from jax.experimental import pallas as pl
from jax.experimental.pallas import tpu as pltpu
from jax.sharding import PartitionSpec as P

MESH = pl.DeviceIdType.MESH
F32 = jnp.float32
BF16 = jnp.bfloat16
SIDE = 4
SUB = 8
LANES = 128
UNROLL = 2
SENDS, RECEIVES = 9, 62


def kernel(
    chips,
    modes,
    taps_len,
    q_in,
    k_in,
    v_in,
    taps_in,
    res_in,
    dec_in,
    w_in,
    g_in,
    proj_out,
    gq_out,
    gk_out,
    gv_out,
    raw,
    taps,
    res,
    dec,
    weight,
    gathered,
    halo,
    extended,
    feats,
    signal,
    conv,
    gradient,
    total_grad,
    filt,
    small,
    rates,
    decay,
    scan_buf,
    prefix,
    s_send,
    s_recv,
    x_send,
    x_recv,
    carry,
    gate,
    keep0,
    keep1,
    send_a,
    send_p,
    send_b,
    recv_a,
    recv_p,
    recv_b,
    part2,
    own2,
    send2_b,
    recv2_a,
    recv2_p,
    recv2_b,
    gfeats,
    edge_send,
    edge_recv,
    to_rows,
    to_tokens,
    local_sem,
    send_sem,
    recv_sem,
    ring_sem,
):
    length, width = q_in.shape
    rows = length // SUB
    half = length // 2
    quarter = length // 4
    ctx = lax.axis_index("ctx")
    ch = lax.axis_index("ch")
    z, core = ctx // 2, ctx % 2
    x, y = ch // SIDE, ch % SIDE
    n_ctx = 2 * chips
    before = (ctx + n_ctx - 1) % n_ctx
    after = (ctx + 1) % n_ctx
    partner = z * 2 + (1 - core)
    place = lax.broadcasted_iota(jnp.int32, (SUB, width), 0)

    def plane(axis, step):
        if axis == 0:
            other = ((x + step) % SIDE) * SIDE + y
        else:
            other = x * SIDE + (y + step) % SIDE
        return {"ctx": ctx, "ch": other}

    def along_z(step):
        return {"ctx": ((z + step) % chips) * 2 + core, "ch": ch}

    def at_ctx(other):
        return {"ctx": other, "ch": ch}

    barrier = pltpu.get_barrier_semaphore()
    peers = [plane(0, 1), plane(0, -1), plane(1, 1), plane(1, -1)]
    peers += [at_ctx(before), at_ctx(after)]
    peers += [along_z(step) for step in (1, -1, 2, -2)]
    for peer in peers:
        pl.semaphore_signal(barrier, inc=1, device_id=peer, device_id_type=MESH)

    local = [
        pltpu.make_async_copy(q_in, raw.at[0], local_sem.at[0]),
        pltpu.make_async_copy(k_in, raw.at[1], local_sem.at[1]),
        pltpu.make_async_copy(v_in, raw.at[2], local_sem.at[2]),
        pltpu.make_async_copy(dec_in, dec, local_sem.at[3]),
        pltpu.make_async_copy(res_in, res, local_sem.at[4]),
        pltpu.make_async_copy(taps_in, taps, local_sem.at[5]),
        pltpu.make_async_copy(g_in, gathered.at[0], local_sem.at[6]),
        pltpu.make_async_copy(w_in, weight, local_sem.at[7]),
    ]
    for copy in local:
        copy.start()
    pl.semaphore_wait(barrier, len(peers))

    slots, sent_on, sent = {}, {}, {}

    def slot_of(name):
        return slots.setdefault(name, len(slots))

    def send(key, group, src, dst, device):
        copy = pltpu.make_async_remote_copy(
            src_ref=src,
            dst_ref=dst,
            send_sem=send_sem.at[sent_on.setdefault(group, len(sent_on))],
            recv_sem=recv_sem.at[slot_of(key)],
            device_id=device,
            device_id_type=MESH,
        )
        sent.setdefault(key, []).append(copy)
        copy.start()

    def receive(*key, view=None):
        if view is None:
            (copy,) = sent[key]
            copy.wait_recv()
        else:
            pltpu.make_async_copy(view, view, recv_sem.at[slots[key]]).wait()

    def slot(h, i, j):
        return gathered.at[i * SIDE + j] if h == 0 else gathered.at[j * SIDE + i]

    def piece(ref, h, part):
        if part is None:
            return ref.at[pl.ds(h * half, half)]
        return ref.at[pl.ds(h * half + part * quarter, quarter)]

    def ag_copy(h, phase, source, i, j, part, step, key=None):
        axis = phase if h == 0 else 1 - phase
        send(
            ("ag", h, i, j, part, step) if key is None else key,
            "ag",
            piece(source, h, part),
            piece(slot(h, i, j), h, part),
            plane(axis, step),
        )

    def ag_wait(h, i, j, part, step):
        receive("ag", h, i, j, part, step)

    for h in range(2):
        for step in (1, -1):
            ag_copy(h, 0, g_in, step % SIDE, 0, None, step)
    for s in range(3):
        tail = (q_in, k_in, v_in)[s].at[pl.ds(length - 16, 16)]
        send(("halo",), "halo", tail, halo.at[s], at_ctx(after))
    for h in range(2):
        for step in (1, -1):
            ag_copy(h, 1, g_in, 0, step % SIDE, None, step)

    def ag_relay1():
        for h in range(2):
            for step in (1, -1):
                i = step % SIDE
                ag_wait(h, i, 0, None, step)
                ag_copy(h, 0, slot(h, i, 0), 2, 0, 0 if step == 1 else 1, step)
        for h in range(2):
            for i in (1, 3):
                for step in (1, -1):
                    ag_copy(h, 1, slot(h, i, 0), i, step % SIDE, None, step)

    def ag_relay2(i):
        for h in range(2):
            for step in (1, -1):
                j = step % SIDE
                ag_wait(h, i, j, None, step)
                ag_copy(h, 1, slot(h, i, j), i, 2, 0 if step == 1 else 1, step, ("last",))

    def ag_far():
        for h in range(2):
            for part, step in ((0, 1), (1, -1)):
                ag_wait(h, 2, 0, part, step)
                for to in (1, -1):
                    key = None if (part == 0) == (to == 1) else ("last",)
                    ag_copy(h, 1, slot(h, 2, 0), 2, to % SIDE, part, to, key)

    def ag_relay_far():
        for h in range(2):
            for step in (1, -1):
                part = 0 if step == 1 else 1
                ag_wait(h, 2, step % SIDE, part, step)
                ag_copy(h, 1, slot(h, 2, step % SIDE), 2, 2, part, step, ("last",))

    reaches = []
    while 2 * 2 ** len(reaches) < chips // 2:
        reaches.append(2 * 2 ** len(reaches))
    news = [0]

    def tell():
        if news[0] < len(reaches):
            for step in (reaches[news[0]], -reaches[news[0]]):
                pl.semaphore_signal(ring_sem.at[news[0]], inc=1, device_id=along_z(step), device_id_type=MESH)

    def pass_news():
        if news[0] < len(reaches):
            pl.semaphore_wait(ring_sem.at[news[0]], 2)
            news[0] += 1
            tell()

    tell()

    def one_hot(hit):
        return jnp.where(hit, 1.0, 0.0).astype(BF16)

    across = lax.broadcasted_iota(jnp.int32, (length, length), 1)
    down = lax.broadcasted_iota(jnp.int32, (length, length), 0)
    to_rows[...] = one_hot(across == (down % SUB) * rows + down // SUB)
    to_tokens[...] = one_hot(down == (across % SUB) * rows + across // SUB)

    def inner_order(value):
        return jnp.dot(to_rows[...], value, preferred_element_type=F32).reshape(rows, SUB, width)

    def token_order(value):
        return jnp.dot(to_tokens[...], value, preferred_element_type=F32).astype(BF16)

    local[3].wait()
    local[4].wait()
    rate = dec[...]
    rates[0] = rate
    rates[1] = res[...] * jnp.sqrt(rate)
    offsets = lax.broadcasted_iota(jnp.int32, (rows, width), 0).astype(F32)
    total = jnp.zeros((rows, width), F32)
    for n in range(modes):
        total = total + rates[1, n : n + 1, :] * jnp.exp(-rates[0, n : n + 1, :] * offsets)
    small[...] = total
    for d in range(rows):
        filt[d] = jnp.broadcast_to(small[d : d + 1, :], (SUB, width))
    for n in range(modes):
        own = jnp.broadcast_to(rates[0, n : n + 1, :], (SUB, width))
        decay[6, n] = jnp.broadcast_to(rates[1, n : n + 1, :], (SUB, width))
        decay[0, n] = jnp.exp(-own)
        step_decay = jnp.exp(-own * rows)
        decay[1, n] = step_decay
        step_decay = step_decay * step_decay
        decay[2, n] = step_decay
        step_decay = step_decay * step_decay
        decay[3, n] = step_decay
        decay[4, n] = jnp.exp(-own * (rows * place).astype(F32))
        decay[5, n] = jnp.exp(-own * (rows * (SUB - 1 - place)).astype(F32))
    block_decay = jnp.exp(-rate * length)
    pair_decay = jnp.exp(-rate * (2 * length))
    sublane = lax.broadcasted_iota(jnp.int32, (modes, SUB, width), 1)
    pass_news()

    def states(signal, direction):
        for lo in range(0, width, LANES):
            cols = slice(lo, lo + LANES)
            step_decay = decay[0, :, :, cols]

            def advance(r, total):
                for k in range(UNROLL):
                    at = UNROLL * r + k if direction == 1 else rows - 1 - k - UNROLL * r
                    total = total * step_decay + signal[at, :, cols][None]
                return total

            scan_buf[:, :, cols] = lax.fori_loop(0, rows // UNROLL, advance, jnp.zeros((modes, SUB, LANES), F32))
        total = scan_buf[...]
        for level, step in enumerate((1, 2, 4)):
            if direction == 1:
                moved = jnp.where(sublane >= step, pltpu.roll(total, step, 1), 0.0)
            else:
                moved = jnp.where(sublane < SUB - step, pltpu.roll(total, SUB - step, 1), 0.0)
            total = total + decay[1 + level] * moved
        if direction == 1:
            prefix[...] = jnp.where(sublane >= 1, pltpu.roll(total, 1, 1), 0.0)
        else:
            prefix[...] = jnp.where(sublane < SUB - 1, pltpu.roll(total, SUB - 1, 1), 0.0)
        scan_buf[...] = total
        edge = SUB - 1 if direction == 1 else 0
        for n in range(modes):
            carry[0, n : n + 1, :] = scan_buf[n, edge : edge + 1, :]

    def send_states(way, direction):
        s_send[way] = carry[0].astype(BF16)
        for step in range(chips // 2, 0, -1):
            for distance in sorted({step, chips - step}):
                send(
                    ("z", way),
                    ("z", way),
                    s_send.at[way],
                    s_recv.at[way, distance - 1],
                    along_z(direction * distance),
                )

    def take_states(way, direction):
        receive("z", way, view=s_recv.at[way])
        total = jnp.zeros((modes, width), F32)
        for distance in range(chips - 1, 0, -1):
            source = z - distance if direction == 1 else chips - 1 - z - distance
            there = (source >= 0).astype(F32)
            total = total * pair_decay + there * s_recv[way, distance - 1].astype(F32)
        leads = (core == 0) if direction == 1 else (core == 1)
        leads = leads.astype(F32)
        x_send[way] = leads * (pair_decay * total + carry[0]) + (1.0 - leads) * total
        send(("x", way), ("x", way), x_send.at[way], x_recv.at[way], at_ctx(partner))
        carry[1] = block_decay * total

    def finish_states(way):
        receive("x", way)
        carry[1] = carry[1] + x_recv[way]
        for n in range(modes):
            scan_buf[n] = jnp.broadcast_to(carry[1, n : n + 1, :], (SUB, width))

    def carried_start(direction):
        reach = decay[4] if direction == 1 else decay[5]
        return decay[6] * decay[0] * (prefix[...] + reach * scan_buf[...])

    def carried(out, start, direction):
        for lo in range(0, width, LANES):
            cols = slice(lo, lo + LANES)
            step_decay = decay[0, :, :, cols]

            def advance(r, state):
                for k in range(UNROLL):
                    at = UNROLL * r + k if direction == 1 else rows - 1 - k - UNROLL * r
                    out[at, :, cols] = out[at, :, cols] + jnp.sum(state, axis=0)
                    state = state * step_decay
                return state

            lax.fori_loop(0, rows // UNROLL, advance, start[:, :, cols])

    for s in range(3):
        local[s].wait()
        extended[s, 8 : 8 + rows] = inner_order(raw[s])
    ag_relay1()
    local[5].wait()
    receive("halo", view=halo)
    first = (ctx > 0).astype(F32)
    for s in range(3):
        small[0:16] = halo[s].astype(F32) * first
        for j in range(1, taps_len):
            moved = pltpu.roll(extended[s, 8 + rows - j], 1, 0)
            extended[s, 8 - j] = jnp.where(
                place == 0, jnp.broadcast_to(small[16 - j : 17 - j, :], (SUB, width)), moved
            )
        total = jnp.zeros((rows, SUB, width), F32)
        for j in range(taps_len):
            total = total + taps[s, j : j + 1, :][None] * extended[s, 8 - j : 8 - j + rows]
        feats[s] = total
    signal[...] = (feats[1] * feats[2]).astype(BF16).astype(F32)

    states(signal, 1)
    while news[0] < len(reaches):
        pass_news()
    send_states(0, 1)
    ag_far()
    ag_relay2(0)

    conv[0] = filt[0][None] * signal[...]
    for d in range(1, rows):
        conv[0, d:rows] = conv[0, d:rows] + filt[d][None] * signal[0 : rows - d]
    ag_relay2(1)
    ag_relay2(3)
    ag_relay_far()

    def grad_terms(blocks):
        total = None
        for dx, dy in blocks:
            source = ((x + SIDE - dx) % SIDE) * SIDE + (y + SIDE - dy) % SIDE
            term = lax.dot_general(
                gathered[dx * SIDE + dy],
                weight[:, pl.ds(pl.multiple_of(source * width, width), width)],
                (((1,), (1,)), ((), ())),
                preferred_element_type=F32,
            )
            total = term if total is None else total + term
        return total

    local[6].wait()
    local[7].wait()
    near = [(dx, dy) for dx in (0, 1, 3) for dy in (0, 1, 3)]
    far = [(dx, dy) for dx in range(SIDE) for dy in range(SIDE) if dx == 2 or dy == 2]
    total_grad[...] = grad_terms(near)

    take_states(0, 1)

    finish_states(0)

    carried(conv.at[0], carried_start(1), 1)
    gate[...] = (feats[0] * conv[0]).astype(BF16).reshape(length, width)

    def rs_copy(key, src, dst, axis, step):
        send(key, "rs", src, dst, plane(axis, step))

    def first_axis(h):
        return 1 if h == 0 else 0

    lower, upper = pl.ds(0, quarter), pl.ds(quarter, quarter)

    def terms(blocks):
        for dx, dy in blocks:
            dest = ((x + dx) % SIDE) * SIDE + (y + dy) % SIDE
            product = jnp.dot(
                gate[...],
                weight[:, pl.ds(pl.multiple_of(dest * width, width), width)],
                preferred_element_type=F32,
            )
            for h in range(2):
                i, j = (dx, dy) if h == 0 else (dy, dx)
                own = product[h * half : (h + 1) * half]
                if j == 2:
                    send_a[h, i] = own.astype(BF16)
                elif j == 1:
                    keep1[h, 0, i] = own[:quarter]
                    send_p[h, 0, i] = own[quarter:].astype(BF16)
                elif j == 3:
                    keep1[h, 1, i] = own[quarter:]
                    send_p[h, 1, i] = own[:quarter].astype(BF16)
                else:
                    keep0[h, i] = own

    def a_copies(*indices):
        for i in indices:
            for h in range(2):
                rs_copy(("a", h, i, 0), send_a.at[h, i, lower], recv_a.at[h, 0, i], first_axis(h), 1)
                rs_copy(("a", h, i, 1), send_a.at[h, i, upper], recv_a.at[h, 1, i], first_axis(h), -1)

    def plain_copies(*indices, ways=(0, 1)):
        for i in indices:
            for h in range(2):
                for way in ways:
                    rs_copy(("pb", h, i), send_p.at[h, way, i], recv_p.at[h, way, i], first_axis(h), 1 - 2 * way)

    def sums_on_the_way(*indices):
        for i in indices:
            for h in range(2):
                for way in range(2):
                    receive("a", h, i, way)
                    send_b[h, way, i] = (keep1[h, way, i] + recv_a[h, way, i].astype(F32)).astype(BF16)
                    rs_copy(("pb", h, i), send_b.at[h, way, i], recv_b.at[h, way, i], first_axis(h), 1 - 2 * way)

    terms(((2, 2),))
    a_copies(2)
    terms(((2, 1), (1, 2)))
    plain_copies(2, ways=(0,))
    a_copies(1)

    receive("last", view=gathered.at[pl.ds(0, 5)])
    grad = total_grad[...] + grad_terms(far)
    high = grad.astype(BF16)
    low = (grad - high.astype(F32)).astype(BF16)
    gradient[...] = inner_order(high) + inner_order(low)
    signal[...] = (gradient[...] * feats[0]).astype(BF16).astype(F32)
    states(signal, -1)
    send_states(1, -1)

    terms(((2, 3), (3, 2)))
    plain_copies(2, ways=(1,))
    a_copies(3)
    terms(((1, 1), (1, 3), (3, 1), (3, 3)))
    plain_copies(1, 3)
    sums_on_the_way(2)
    sums_on_the_way(1, 3)
    terms(((2, 0), (0, 2)))
    a_copies(0)
    terms(((0, 1), (1, 0), (0, 3), (3, 0), (0, 0)))
    plain_copies(0)

    def edges(s, key):
        for j in range(16):
            small[j : j + 1, :] = gfeats[s, j, 0:1, :]
        edge_send[s] = small[0:16].astype(BF16)
        send(key, key, edge_send.at[s], edge_recv.at[s], at_ctx(before))

    gfeats[0, 0:rows] = (gradient[...] * conv[0]).astype(BF16).astype(F32)
    edges(0, ("edge", 0))
    conv[1] = filt[0][None] * signal[...]
    for d in range(1, rows):
        conv[1, 0 : rows - d] = conv[1, 0 : rows - d] + filt[d][None] * signal[d:rows]

    def collect(h, i):
        receive("pb", h, i, view=send_a.at[h, pl.ds(0, 2)])
        low = keep0[h, i, 0:quarter] + recv_b[h, 0, i].astype(F32) + recv_p[h, 1, i].astype(F32)
        high = keep0[h, i, quarter:half] + recv_p[h, 0, i].astype(F32) + recv_b[h, 1, i].astype(F32)
        return low, high

    for h in range(2):
        axis = 1 - first_axis(h)
        low, high = collect(h, 2)
        part2[h, 0] = low.astype(BF16)
        part2[h, 1] = high.astype(BF16)
        rs_copy(("a2", h, 0), part2.at[h, 0], recv2_a.at[h, 0], axis, 1)
        rs_copy(("a2", h, 1), part2.at[h, 1], recv2_a.at[h, 1], axis, -1)
    sums_on_the_way(0)

    last = (ctx < n_ctx - 1).astype(F32)

    def featurize_back(s):
        small[0:16] = edge_recv[s].astype(F32) * last
        for j in range(taps_len - 1):
            moved = pltpu.roll(gfeats[s, j], SUB - 1, 0)
            gfeats[s, rows + j] = jnp.where(
                place == SUB - 1, jnp.broadcast_to(small[j : j + 1, :], (SUB, width)), moved
            )
        total = jnp.zeros((rows, SUB, width), F32)
        for j in range(taps_len):
            total = total + taps[s, j : j + 1, :][None] * gfeats[s, j : j + rows]
        (gq_out, gk_out, gv_out)[s][...] = token_order(total.astype(BF16).reshape(length, width))

    take_states(1, -1)

    for h in range(2):
        axis = 1 - first_axis(h)
        low, high = collect(h, 1)
        own2[h, 0] = low
        part2[h, 2] = high.astype(BF16)
        rs_copy(("pb2", h), part2.at[h, 2], recv2_p.at[h, 0], axis, 1)
        low, high = collect(h, 3)
        own2[h, 1] = high
        part2[h, 3] = low.astype(BF16)
        rs_copy(("pb2", h), part2.at[h, 3], recv2_p.at[h, 1], axis, -1)
        for way in range(2):
            receive("a2", h, way)
            send2_b[h, way] = (own2[h, way] + recv2_a[h, way].astype(F32)).astype(BF16)
            rs_copy(("pb2", h), send2_b.at[h, way], recv2_b.at[h, way], axis, 1 - 2 * way)

    finish_states(1)
    carried(conv.at[1], carried_start(-1), -1)
    gfeats[1, 0:rows] = (conv[1] * feats[2]).astype(BF16).astype(F32)
    edges(1, ("edge", 1))
    gfeats[2, 0:rows] = (conv[1] * feats[1]).astype(BF16).astype(F32)
    edges(2, ("edge", 1))
    receive("edge", 0)
    featurize_back(0)
    for h in range(2):
        low, high = collect(h, 0)
        own2[h, 2] = low
        own2[h, 3] = high

    receive("edge", 1, view=edge_recv.at[pl.ds(0, 2)])
    featurize_back(1)
    featurize_back(2)

    for h in range(2):
        receive("pb2", h, view=send_a.at[h, pl.ds(0, 2)])
        low = own2[h, 2] + recv2_b[h, 0].astype(F32) + recv2_p[h, 1].astype(F32)
        high = own2[h, 3] + recv2_p[h, 0].astype(F32) + recv2_b[h, 1].astype(F32)
        gate[h * half : h * half + quarter] = low.astype(BF16)
        gate[h * half + quarter : (h + 1) * half] = high.astype(BF16)
    proj_out[...] = token_order(gate[...])

    views = {
        "ag": gathered.at[pl.ds(0, SIDE * SIDE - 1)],
        "rs": gathered.at[pl.ds(0, SIDE * SIDE - 1)],
        "halo": halo,
        ("z", 0): s_recv.at[0],
        ("z", 1): s_recv.at[1],
        ("x", 0): x_recv.at[0],
        ("x", 1): x_recv.at[1],
        ("edge", 0): edge_recv.at[0],
        ("edge", 1): edge_recv.at[pl.ds(0, 2)],
    }
    assert (len(sent_on), len(slots)) == (SENDS, RECEIVES)
    for group, index in sent_on.items():
        pltpu.make_async_copy(views[group], views[group], send_sem.at[index]).wait()


def deliver(*refs):
    sources, targets, sem = refs[:4], refs[4:8], refs[8]
    copies = [pltpu.make_async_copy(sources[i], targets[i], sem.at[i]) for i in range(4)]
    for copy in copies:
        copy.start()
    for copy in copies:
        copy.wait()


def shards(query_in, key_in, value_in, short_taps, residues, decays, out_weight, out_grad):
    length, width = query_in.shape
    rows = length // SUB
    half, quarter = length // 2, length // 4
    short_taps = jnp.transpose(short_taps, (1, 0, 2))
    residues, decays = residues.T, decays.T
    taps_len = short_taps.shape[1]
    modes = decays.shape[0]
    chips = lax.axis_size("ctx") // 2
    vmem = pltpu.VMEM
    dma = pltpu.SemaphoreType.DMA
    scratch = [
        vmem((3, length, width), BF16),
        vmem(short_taps.shape, F32),
        vmem(residues.shape, F32),
        vmem(decays.shape, F32),
        vmem(out_weight.shape, BF16),
        vmem((SIDE * SIDE, length, width), BF16),
        vmem((3, 16, width), BF16),
        vmem((3, rows + 8, SUB, width), F32),
        vmem((3, rows, SUB, width), F32),
        vmem((rows, SUB, width), F32),
        vmem((2, rows, SUB, width), F32),
        vmem((rows, SUB, width), F32),
        vmem((length, width), F32),
        vmem((rows, SUB, width), F32),
        vmem((rows, width), F32),
        vmem((2, modes, width), F32),
        vmem((7, modes, SUB, width), F32),
        vmem((modes, SUB, width), F32),
        vmem((modes, SUB, width), F32),
        vmem((2, modes, width), BF16),
        vmem((2, chips - 1, modes, width), BF16),
        vmem((2, modes, width), F32),
        vmem((2, modes, width), F32),
        vmem((2, modes, width), F32),
        vmem((length, width), BF16),
        vmem((2, SIDE, half, width), F32),
        vmem((2, 2, SIDE, quarter, width), F32),
        vmem((2, SIDE, half, width), BF16),
        vmem((2, 2, SIDE, quarter, width), BF16),
        vmem((2, 2, SIDE, quarter, width), BF16),
        vmem((2, 2, SIDE, quarter, width), BF16),
        vmem((2, 2, SIDE, quarter, width), BF16),
        vmem((2, 2, SIDE, quarter, width), BF16),
        vmem((2, 4, quarter, width), BF16),
        vmem((2, 4, quarter, width), F32),
        vmem((2, 2, quarter, width), BF16),
        vmem((2, 2, quarter, width), BF16),
        vmem((2, 2, quarter, width), BF16),
        vmem((2, 2, quarter, width), BF16),
        vmem((3, rows + 8, SUB, width), F32),
        vmem((3, 16, width), BF16),
        vmem((3, 16, width), BF16),
        vmem((length, length), BF16),
        vmem((length, length), BF16),
        dma((8,)),
        dma((SENDS,)),
        dma((RECEIVES,)),
        pltpu.SemaphoreType.REGULAR((2,)),
    ]
    out = jax.ShapeDtypeStruct((length, width), BF16)
    results = pl.pallas_call(
        functools.partial(kernel, chips, modes, taps_len),
        out_shape=(pltpu.VMEM((length, width), BF16),) * 4,
        in_specs=[pl.BlockSpec(memory_space=pl.ANY)] * 8,
        out_specs=[pl.BlockSpec(memory_space=pltpu.VMEM)] * 4,
        scratch_shapes=scratch,
        compiler_params=pltpu.CompilerParams(
            collective_id=0, has_side_effects=True, vmem_limit_bytes=56 * 1024 * 1024
        ),
        name="hyena",
    )(query_in, key_in, value_in, short_taps, residues, decays, out_weight, out_grad)
    return pl.pallas_call(
        deliver,
        out_shape=(out, out, out, out),
        in_specs=[pl.BlockSpec(memory_space=pltpu.VMEM)] * 4,
        out_specs=[pl.BlockSpec(memory_space=pl.ANY)] * 4,
        scratch_shapes=[dma((4,))],
        name="deliver",
    )(*[pltpu.with_memory_space_constraint(r, pltpu.VMEM) for r in results])


def solution(mesh):
    in_specs = (
        P("ctx", "ch"),
        P("ctx", "ch"),
        P("ctx", "ch"),
        P(None, None, "ch"),
        P("ch", None),
        P("ch", None),
        P("ch", None),
        P("ctx", "ch"),
    )
    out_specs = (P("ctx", "ch"), P("ctx", "ch"), P("ctx", "ch"), P("ctx", "ch"))
    return jax.shard_map(shards, mesh=mesh, in_specs=in_specs, out_specs=out_specs, check_vma=False)
```
